512 devices in a mesh: rows: 128 (over y_hi, z, x), cols: 4 (over y_lo, core).
Axes of the slice: x: 4, y: 4 (y_hi: 2, y_lo: 2; y = y_hi * 2 + y_lo), z: 16, core: 2. Of those that a mesh axis runs over, the one named last changes fastest.
Arguments:
- features: bfloat16 [524288, 256], P('rows', 'cols'), may hold values from -6 to 6
- weight: bfloat16 [256, 256], P(None, 'cols'), may hold values from -0.375 to 0.375
- tile_values: bfloat16 [11264, 128, 128], P('rows'), as said below
- tile_rows: int32 [11264], P('rows'), may hold values from 0 to 31
- tile_cols: int32 [11264], P('rows'), may hold values from 0 to 159, as said below
- tile_count: int32 [128], P('rows'), may hold values from 44 to 88, as said below
- cotangent: bfloat16 [524288, 256], P('rows', 'cols'), may hold values from -6 to 6
Outputs:
- output: bfloat16 [524288, 256], P('rows', 'cols')
- feature_grad: bfloat16 [524288, 256], P('rows', 'cols')
- weight_grad: float32 [256, 256], P(None, 'cols')
The draws below stay inside these ranges and needn't reach their ends.
Inputs may be any that keep to these rules, and one draw needn't show every extreme that they name: `tile_count`: live tile slots of a partition, at least 44; some partition has all 88 slots live in every draw. `tile_cols`: slot s of a partition (counted from the partition's first slot) draws its source from the partition (s mod 5) - 2 steps away around the loop, so c div (32) = s mod 5. `tile_values`: edge weights are zero or positive.
All inputs are finite; a program needn't handle non-finite values.
Results may differ from the reference program's by a relative error of at most 0.02.
Values may be sent and summed in bfloat16 or wider, within the bound.
No kernel may reach another device: no remote copies, remote signals or barrier semaphores. Data moves between devices by JAX's collectives and lax.ppermute only.
A program may use at most 64 MiB of HBM per device.

```python
import math
import jax
import jax.numpy as jnp
from jax import lax

FEAT = 256
TILE = 128
NODE_DEV = 4096
NT = 88
NODES = 524288
TILES = 11264
N_ROWS = 128
N_COLS = 4


def draw_tile_values(key, part):
    mask_key = jax.random.fold_in(key, 11)
    size_key = jax.random.fold_in(key, 12)
    shape = (TILES, TILE, TILE)
    present = jax.random.bernoulli(mask_key, 0.5, shape).astype(jnp.float32)
    sizes = jnp.exp(jax.random.uniform(size_key, shape, jnp.float32, math.log(0.5), math.log(2.0)))
    return (present * sizes * (1.0 / math.sqrt(TILE))).astype(jnp.bfloat16)


def draw_tile_rows(key, part):
    return jax.random.randint(jax.random.fold_in(key, 21), (TILES,), 0, NODE_DEV // TILE).astype(jnp.int32)


def draw_tile_cols(key, part):
    slot_ids = jnp.arange(TILES, dtype=jnp.int32) % NT
    offset_ids = slot_ids % 5
    block_ids = jax.random.randint(jax.random.fold_in(key, 31), (TILES,), 0, NODE_DEV // TILE).astype(jnp.int32)
    return (offset_ids * (NODE_DEV // TILE) + block_ids).astype(jnp.int32)


def draw_tile_count(key, part):
    counts = jax.random.randint(jax.random.fold_in(key, 41), (N_ROWS,), NT // 2, NT + 1).astype(jnp.int32)
    fullest = jax.random.randint(jax.random.fold_in(key, 42), (), 0, N_ROWS)
    return counts.at[fullest].set(NT).astype(jnp.int32)


def block_scale(rng, extent, pieces, smallest, largest):
    def one(position, shards_of):
        steps = jax.random.uniform(jax.random.fold_in(jax.random.fold_in(rng, 6), position), (shards_of,), jnp.float32, smallest / len(pieces), largest / len(pieces))
        return jnp.repeat(jnp.exp(steps), extent[position] // shards_of).reshape((-1,) + (1,) * (len(extent) - position - 1))

    level = one(*pieces[0])
    for cut in pieces[1:]:
        level = level * one(*cut)
    return level


def scatter_about(stream_key, dims, scale, most, shards=(), kind=jnp.bfloat16):
    values = jax.random.normal(stream_key, dims, jnp.float32) * scale
    if len(shards) > 0:
        values = block_scale(stream_key, dims, shards, -0.22, 0.18) * values
    return jnp.clip(values, min=-most, max=most).astype(kind)


def setup_inputs(seed: int = 0) -> dict:
    keys = jax.random.split(jax.random.key(seed), 8)
    return {
        "features": scatter_about(keys[0], (NODES, FEAT), 1.0, 6.0, ((0, 128), (1, 4))),
        "weight": scatter_about(keys[1], (FEAT, FEAT), FEAT ** -0.5, 0.375, ((1, 4),)),
        "tile_values": draw_tile_values(jax.random.fold_in(keys[7], 71), 0),
        "tile_rows": draw_tile_rows(jax.random.fold_in(keys[7], 71), 0),
        "tile_cols": draw_tile_cols(jax.random.fold_in(keys[7], 71), 0),
        "tile_count": draw_tile_count(jax.random.fold_in(keys[7], 71), 0),
        "cotangent": scatter_about(keys[6], (NODES, FEAT), 1.0, 6.0, ((0, 128), (1, 4))),
    }


def silu_grad(value):
    sigmoid_val = jax.nn.sigmoid(value)
    return sigmoid_val * (1.0 + value * (1.0 - sigmoid_val))

def reference(features, weight, tile_values, tile_rows, tile_cols, tile_count, cotangent):
    block_count = NODE_DEV // TILE
    feature_view = features.reshape(N_ROWS, NODE_DEV, FEAT)
    tile_view = tile_values.reshape(N_ROWS, NT, TILE, TILE)
    row_view = tile_rows.reshape(N_ROWS, NT)
    col_view = tile_cols.reshape(N_ROWS, NT)
    slot_ids = jnp.arange(NT, dtype=jnp.int32)
    offsets = jnp.arange(5, dtype=jnp.int32) - 2
    dest_ids = jnp.arange(block_count, dtype=jnp.int32)
    band_ids = jnp.arange(5 * block_count, dtype=jnp.int32)

    def aggregate(index_row):
        owners = (index_row + offsets) % N_ROWS
        band_rows = feature_view[owners].reshape(5 * block_count, TILE, FEAT)
        tiles = tile_view[index_row].astype(jnp.float32)
        live_slots = (slot_ids < tile_count[index_row]).astype(jnp.float32)
        source = band_rows[col_view[index_row]].astype(jnp.float32)
        products = jnp.einsum('tij,tjf->tif', tiles, source) * live_slots[:, None, None]
        row_select = (row_view[index_row][None, :] == dest_ids[:, None]).astype(jnp.float32)
        return jnp.einsum('bt,tif->bif', row_select, products).reshape(NODE_DEV, FEAT)
    hidden = lax.map(aggregate, jnp.arange(N_ROWS, dtype=jnp.int32)).reshape(NODES, FEAT).astype(jnp.bfloat16)
    preact = jnp.dot(hidden, weight, preferred_element_type=jnp.float32)
    output = jax.nn.silu(preact).astype(jnp.bfloat16)
    grad_pre = (cotangent.astype(jnp.float32) * silu_grad(preact)).astype(jnp.bfloat16)
    weight_grad = jnp.dot(hidden.T, grad_pre, preferred_element_type=jnp.float32) * (1.0 / math.sqrt(NODES))
    width = FEAT // N_COLS
    summed = jnp.zeros((NODES, FEAT), jnp.float32)
    for group in range(N_COLS):
        piece = jnp.dot(grad_pre[:, group * width:(group + 1) * width], weight[:, group * width:(group + 1) * width].T, preferred_element_type=jnp.float32).astype(jnp.bfloat16)
        piece = lax.optimization_barrier(piece)
        summed = summed + piece.astype(jnp.float32)
    hidden_grad = summed.astype(jnp.bfloat16)
    grad_blocks = hidden_grad.reshape(N_ROWS, block_count, TILE, FEAT)

    def spread(gathered, index_row):
        tiles = tile_view[index_row].astype(jnp.float32)
        live_slots = (slot_ids < tile_count[index_row]).astype(jnp.float32)
        source = grad_blocks[index_row][row_view[index_row]].astype(jnp.float32)
        contrib = jnp.einsum('tji,tjf->tif', tiles, source) * live_slots[:, None, None]
        band_select = (col_view[index_row][None, :] == band_ids[:, None]).astype(jnp.float32)
        outgoing = jnp.einsum('ct,tif->cif', band_select, contrib).reshape(5, NODE_DEV, FEAT)
        owners = (index_row + offsets) % N_ROWS
        return (gathered.at[owners].add(outgoing), None)
    start = jnp.zeros((N_ROWS, NODE_DEV, FEAT), jnp.float32)
    gathered, unused = lax.scan(spread, start, jnp.arange(N_ROWS, dtype=jnp.int32))
    feature_grad = gathered.reshape(NODES, FEAT).astype(jnp.bfloat16)
    return (output, feature_grad, weight_grad)
```

```python
import jax
import jax.numpy as jnp
from jax import lax
from jax.experimental import pallas as pl
from jax.experimental.pallas import tpu as pltpu
from jax.sharding import Mesh, PartitionSpec as P

ROWS = ("yh", "z", "x")
COLS = ("yl", "core")
BLOCK = 128
NEAR = 5
VMEM = pl.BlockSpec(memory_space=pltpu.VMEM)
SMEM = pl.BlockSpec(memory_space=pltpu.SMEM)
BATCH = 6


def swap_pairs(count, odd):
    pairs = []
    for first in range(odd, count, 2):
        second = (first + 1) % count
        pairs += [(first, second), (second, first)]
    return pairs


def lanes(index):
    return pl.ds(pl.multiple_of(index * BLOCK, BLOCK), BLOCK)


def each_tile(offset, count, values_ref, term, add):
    slots = values_ref.shape[0]
    per_offset = -(-slots // NEAR)
    for first in range(0, per_offset, BATCH):
        held = []
        for k in range(first, min(first + BATCH, per_offset)):
            slot = k * NEAR + offset
            live = (slot < count).astype(jnp.float32)
            slot = jnp.minimum(slot, slots - 1)
            held.append((slot, term(slot) * live))
        for slot, product in held:
            add(slot, product)


def gather_terms(info, source_ref, total_ref, offset):
    values_ref, rows_ref, cols_ref, count = info
    blocks = source_ref.shape[1] // BLOCK

    def term(slot):
        source = source_ref[:, lanes(lax.rem(cols_ref[slot], blocks))]
        return lax.dot_general(
            source, values_ref[slot], (((1,), (1,)), ((), ())), preferred_element_type=jnp.float32
        )

    def add(slot, product):
        where = lanes(rows_ref[slot])
        total_ref[:, where] = total_ref[:, where] + product

    each_tile(offset, count, values_ref, term, add)


def near_kernel(values, rows, cols, count, parity, own, even, odd, total):
    total[...] = jnp.zeros_like(total)
    info = (values, rows, cols, count[0])
    even_offset = 3 - 2 * parity[0]
    gather_terms(info, own, total, 2)
    gather_terms(info, even, total, even_offset)
    gather_terms(info, odd, total, 4 - even_offset)


def far_kernel(values, rows, cols, count, parity, start, even, odd, hidden, total):
    total[...] = start[...]
    info = (values, rows, cols, count[0])
    even_offset = 4 - 4 * parity[0]
    gather_terms(info, even, total, even_offset)
    gather_terms(info, odd, total, 4 - even_offset)
    parts, _, width = hidden.shape
    for part in range(parts):
        hidden[part] = total[:, part * width : (part + 1) * width].astype(hidden.dtype)


def dense_kernel(hidden, cotangent, weight_t, weight, output, hidden_grad, grad_pre):
    parts, cols, width = hidden.shape
    full = parts * cols
    source = hidden[...].reshape(full, width)
    preact = jnp.dot(weight_t[...], source, preferred_element_type=jnp.float32)
    sigmoid = 1.0 / (1.0 + jnp.exp(-preact))
    output[...] = (preact * sigmoid).astype(output.dtype).reshape(output.shape)
    slope = sigmoid * (1.0 + preact * (1.0 - sigmoid))
    grad = cotangent[...].reshape(full, width).astype(jnp.float32) * slope
    grad = grad.astype(jnp.bfloat16)
    grad_pre[...] = grad
    back = jnp.dot(weight[...], grad, preferred_element_type=jnp.float32)
    hidden_grad[...] = back.astype(hidden_grad.dtype).reshape(hidden_grad.shape)


def spread_terms(info, grad_ref, total_ref, offset):
    values_ref, rows_ref, cols_ref, count = info
    parts, _, width = grad_ref.shape
    blocks = parts * width // BLOCK
    per_part = width // BLOCK

    def term(slot):
        row = rows_ref[slot]
        part = row // per_part
        source = grad_ref[part, :, lanes(row - part * per_part)]
        return jnp.dot(source, values_ref[slot], preferred_element_type=jnp.float32)

    def add(slot, product):
        where = lanes(lax.rem(cols_ref[slot], blocks))
        total_ref[:, where] = total_ref[:, where] + product

    each_tile(offset, count, values_ref, term, add)


def spread_far_kernel(values, rows, cols, count, parity, grad, even, odd, even_total, odd_total):
    info = (values, rows, cols, count[0])
    even_offset = 4 - 4 * parity[0]
    for offset, total, out in ((even_offset, even_total, even), (4 - even_offset, odd_total, odd)):
        total[...] = jnp.zeros_like(total)
        spread_terms(info, grad, total, offset)
        out[...] = total[...].astype(out.dtype)


def spread_near_kernel(values, rows, cols, count, parity, grad, even, odd, own):
    info = (values, rows, cols, count[0])
    even_offset = 3 - 2 * parity[0]
    for offset, total in ((even_offset, even), (4 - even_offset, odd), (2, own)):
        total[...] = jnp.zeros_like(total)
        spread_terms(info, grad, total, offset)


def call(kernel, args, specs, outs, scratch=(), flops=0):
    moved = sum(a.size * a.dtype.itemsize for a in args)
    moved += sum(o.size * o.dtype.itemsize for o in outs)
    return pl.pallas_call(
        kernel,
        out_shape=outs,
        in_specs=specs,
        out_specs=[VMEM] * len(outs),
        scratch_shapes=scratch,
        cost_estimate=pl.CostEstimate(flops=flops, bytes_accessed=moved, transcendentals=0),
        compiler_params=pltpu.CompilerParams(vmem_limit_bytes=24 << 20),
    )(*args)


def swapped(value):
    return lax.all_to_all(value, COLS, 0, 0, tiled=True)


def local(features, weight, tile_values, tile_rows, tile_cols, tile_count, cotangent):
    node_count, feat_cols = features.shape
    slots, tile, _ = tile_values.shape
    n_rows = lax.axis_size(ROWS)
    n_cols = lax.axis_size(COLS)
    width = node_count // n_cols
    full = feat_cols * n_cols
    even_pairs = swap_pairs(n_rows, 0)
    odd_pairs = swap_pairs(n_rows, 1)

    def even_swap(value):
        return lax.ppermute(value, ROWS, even_pairs)

    def odd_swap(value):
        return lax.ppermute(value, ROWS, odd_pairs)

    def pieces(value):
        return value.reshape(feat_cols, n_cols, width).transpose(1, 0, 2)

    parity = lax.rem(lax.axis_index("x"), 2).astype(jnp.int32).reshape(1)
    tables = (tile_values, tile_rows, tile_cols, tile_count, parity)
    table_specs = [VMEM, SMEM, SMEM, SMEM, SMEM]
    tile_flops = 2 * tile * tile * feat_cols
    wide = jax.ShapeDtypeStruct((feat_cols, node_count), jnp.float32)
    sent = jax.ShapeDtypeStruct((feat_cols, node_count), jnp.bfloat16)
    piece = jax.ShapeDtypeStruct((n_cols, feat_cols, width), jnp.bfloat16)
    total = pltpu.VMEM((feat_cols, node_count), jnp.float32)

    own = features.T
    even1 = even_swap(own)
    odd1 = odd_swap(own)
    weight_t = lax.all_gather(weight.T, COLS, axis=0, tiled=True)
    grad_out = swapped(pieces(cotangent.T))
    even1, odd1, weight_t = lax.optimization_barrier((even1, odd1, weight_t))
    odd2 = odd_swap(even1)
    even2 = even_swap(odd1)
    (near,) = call(
        near_kernel, tables + (own, even1, odd1), table_specs + [VMEM] * 3, [wide], flops=54 * tile_flops
    )
    (hidden,) = call(
        far_kernel,
        tables + (near, even2, odd2),
        table_specs + [VMEM] * 3,
        [piece],
        scratch=[total],
        flops=36 * tile_flops,
    )
    hidden = swapped(hidden)
    output, hidden_grad, grad_pre = call(
        dense_kernel,
        (hidden, grad_out, weight_t, weight_t.T),
        [VMEM] * 4,
        [piece, piece, jax.ShapeDtypeStruct((full, width), jnp.bfloat16)],
        flops=4 * full * full * width,
    )
    hidden_grad = swapped(hidden_grad)
    even_far, odd_far = call(
        spread_far_kernel,
        tables + (hidden_grad,),
        table_specs + [VMEM],
        [sent, sent],
        scratch=[total, total],
        flops=36 * tile_flops,
    )
    even_in = even_swap(even_far)
    odd_in = odd_swap(odd_far)
    even_near, odd_near, kept = call(
        spread_near_kernel,
        tables + (hidden_grad,),
        table_specs + [VMEM],
        [wide, wide, wide],
        flops=54 * tile_flops,
    )
    kept, grad_pre, hidden = lax.optimization_barrier((kept, grad_pre, hidden))
    weight_term = lax.dot_general(
        grad_pre,
        hidden.reshape(full, width),
        (((1,), (1,)), ((), ())),
        preferred_element_type=jnp.float32,
    )
    weight_term = swapped(weight_term.reshape(n_cols, feat_cols, full)).sum(0)
    even_near, odd_near, weight_term, output = lax.optimization_barrier(
        (even_near, odd_near, weight_term, output)
    )
    odd_last = (odd_near + even_in.astype(jnp.float32)).astype(jnp.bfloat16)
    even_last = (even_near + odd_in.astype(jnp.float32)).astype(jnp.bfloat16)
    odd_last, even_last, weight_term = lax.optimization_barrier((odd_last, even_last, weight_term))
    odd_last = odd_swap(odd_last)
    even_last = even_swap(even_last)
    weight_term = lax.all_gather(weight_term, "x").sum(0)
    halves = lax.all_gather(weight_term[:32], "z"), lax.all_gather(weight_term[32:], "z")
    weight_term = jnp.concatenate([half.sum(0) for half in halves], 0)
    weight_term = weight_term + lax.ppermute(weight_term, "yh", swap_pairs(2, 0))
    weight_grad = (weight_term * (1.0 / (node_count * n_rows) ** 0.5)).T

    output = swapped(output).transpose(1, 0, 2).reshape(feat_cols, node_count).T
    gathered = kept + even_last.astype(jnp.float32) + odd_last.astype(jnp.float32)
    feature_grad = gathered.astype(jnp.bfloat16).T
    return (output, feature_grad, weight_grad)


def solution(mesh):
    n_rows, n_cols = mesh.shape["rows"], mesh.shape["cols"]
    devices = mesh.devices.reshape(2, n_rows // 8, 4, 2, n_cols // 2)
    fine = Mesh(devices, ROWS + COLS)
    in_specs = (
        P(ROWS, COLS),
        P(None, COLS),
        P(ROWS, None, None),
        P(ROWS),
        P(ROWS),
        P(ROWS),
        P(ROWS, COLS),
    )
    out_specs = (P(ROWS, COLS), P(ROWS, COLS), P(None, COLS))
    return jax.shard_map(local, mesh=fine, in_specs=in_specs, out_specs=out_specs, check_vma=False)
```

```python
import jax
import jax.numpy as jnp
from jax import lax
from jax.experimental import pallas as pl
from jax.experimental.pallas import tpu as pltpu
from jax.sharding import Mesh, PartitionSpec as P

ROWS = ("yh", "zh", "zl", "x")
COLS = ("yl", "core")
BLOCK = 128
NEAR = 5
VMEM = pl.BlockSpec(memory_space=pltpu.VMEM)
SMEM = pl.BlockSpec(memory_space=pltpu.SMEM)
BATCH = 6


def swap_pairs(count, odd):
    pairs = []
    for first in range(odd, count, 2):
        second = (first + 1) % count
        pairs += [(first, second), (second, first)]
    return pairs


def lanes(index):
    return pl.ds(pl.multiple_of(index * BLOCK, BLOCK), BLOCK)


def each_tile(offset, count, values_ref, term, add):
    slots = values_ref.shape[0]
    per_offset = -(-slots // NEAR)
    for first in range(0, per_offset, BATCH):
        held = []
        for k in range(first, min(first + BATCH, per_offset)):
            slot = k * NEAR + offset
            live = (slot < count).astype(jnp.float32)
            slot = jnp.minimum(slot, slots - 1)
            held.append((slot, term(slot) * live))
        for slot, product in held:
            add(slot, product)


def gather_terms(info, source_ref, total_ref, offset):
    values_ref, rows_ref, cols_ref, count = info
    blocks = source_ref.shape[1] // BLOCK

    def term(slot):
        source = source_ref[:, lanes(lax.rem(cols_ref[slot], blocks))]
        return lax.dot_general(
            source, values_ref[slot], (((1,), (1,)), ((), ())), preferred_element_type=jnp.float32
        )

    def add(slot, product):
        where = lanes(rows_ref[slot])
        total_ref[:, where] = total_ref[:, where] + product

    each_tile(offset, count, values_ref, term, add)


def near_kernel(values, rows, cols, count, parity, own, even, odd, total):
    total[...] = jnp.zeros_like(total)
    info = (values, rows, cols, count[0])
    even_offset = 3 - 2 * parity[0]
    gather_terms(info, own, total, 2)
    gather_terms(info, even, total, even_offset)
    gather_terms(info, odd, total, 4 - even_offset)


def far_kernel(values, rows, cols, count, parity, start, even, odd, hidden, total):
    total[...] = start[...]
    info = (values, rows, cols, count[0])
    even_offset = 4 - 4 * parity[0]
    gather_terms(info, even, total, even_offset)
    gather_terms(info, odd, total, 4 - even_offset)
    parts, _, width = hidden.shape
    for part in range(parts):
        hidden[part] = total[:, part * width : (part + 1) * width].astype(hidden.dtype)


def dense_kernel(hidden, given, output, sent):
    parts, cols, width = hidden.shape
    full = parts * cols
    source = hidden[...].reshape(full, width)
    weight_t = given[:, :, width:].reshape(full, full)
    preact = jnp.dot(weight_t, source, preferred_element_type=jnp.float32)
    sigmoid = 1.0 / (1.0 + jnp.exp(-preact))
    output[...] = (preact * sigmoid).astype(output.dtype).reshape(output.shape)
    slope = sigmoid * (1.0 + preact * (1.0 - sigmoid))
    grad = given[:, :, :width].reshape(full, width).astype(jnp.float32) * slope
    grad = grad.astype(jnp.bfloat16)
    back = lax.dot_general(
        weight_t, grad, (((0,), (0,)), ((), ())), preferred_element_type=jnp.float32
    )
    sent[:, :, :width] = back.astype(sent.dtype).reshape(parts, cols, width)
    weight_term = lax.dot_general(
        grad, source, (((1,), (1,)), ((), ())), preferred_element_type=jnp.float32
    )
    sent[:, :, width:] = weight_term.astype(sent.dtype).reshape(parts, cols, full)


def spread_terms(info, grad_ref, total_ref, offset):
    values_ref, rows_ref, cols_ref, count = info
    blocks = total_ref.shape[1] // BLOCK
    per_part = blocks // grad_ref.shape[0]

    def term(slot):
        row = rows_ref[slot]
        part = row // per_part
        source = grad_ref[part, :, lanes(row - part * per_part)]
        return jnp.dot(source, values_ref[slot], preferred_element_type=jnp.float32)

    def add(slot, product):
        where = lanes(lax.rem(cols_ref[slot], blocks))
        total_ref[:, where] = total_ref[:, where] + product

    each_tile(offset, count, values_ref, term, add)


def spread_far_kernel(values, rows, cols, count, parity, grad, even, odd, even_total, odd_total):
    info = (values, rows, cols, count[0])
    even_offset = 4 - 4 * parity[0]
    for offset, total, out in ((even_offset, even_total, even), (4 - even_offset, odd_total, odd)):
        total[...] = jnp.zeros_like(total)
        spread_terms(info, grad, total, offset)
        out[...] = total[...].astype(out.dtype)


def spread_near_kernel(
    values, rows, cols, count, parity, grad, from_odd, from_even, even, odd, even_total, odd_total
):
    info = (values, rows, cols, count[0])
    even_offset = 3 - 2 * parity[0]
    for offset, start, total, out in (
        (even_offset, from_odd, even_total, even),
        (4 - even_offset, from_even, odd_total, odd),
    ):
        total[...] = start[...].astype(total.dtype)
        spread_terms(info, grad, total, offset)
        out[...] = total[...].astype(out.dtype)


def spread_own_kernel(values, rows, cols, count, parity, grad, from_even, from_odd, out, total):
    info = (values, rows, cols, count[0])
    total[...] = from_even[...].astype(total.dtype) + from_odd[...].astype(total.dtype)
    spread_terms(info, grad, total, 2)
    out[...] = total[...].astype(out.dtype)


def call(kernel, args, specs, outs, scratch=(), flops=0):
    moved = sum(a.size * a.dtype.itemsize for a in args)
    moved += sum(o.size * o.dtype.itemsize for o in outs)
    return pl.pallas_call(
        kernel,
        out_shape=outs,
        in_specs=specs,
        out_specs=[VMEM] * len(outs),
        scratch_shapes=scratch,
        cost_estimate=pl.CostEstimate(flops=flops, bytes_accessed=moved, transcendentals=0),
        compiler_params=pltpu.CompilerParams(vmem_limit_bytes=24 << 20),
    )(*args)


def swapped(value):
    return lax.all_to_all(value, COLS, 0, 0, tiled=True)


def local(features, weight, tile_values, tile_rows, tile_cols, tile_count, cotangent):
    node_count, feat_cols = features.shape
    slots, tile, _ = tile_values.shape
    n_rows = lax.axis_size(ROWS)
    n_cols = lax.axis_size(COLS)
    width = node_count // n_cols
    full = feat_cols * n_cols
    even_pairs = swap_pairs(n_rows, 0)
    odd_pairs = swap_pairs(n_rows, 1)

    def even_swap(value):
        return lax.ppermute(value, ROWS, even_pairs)

    def odd_swap(value):
        return lax.ppermute(value, ROWS, odd_pairs)

    def pieces(value):
        return value.reshape(feat_cols, n_cols, width).transpose(1, 0, 2)

    parity = lax.rem(lax.axis_index("x"), 2).astype(jnp.int32).reshape(1)
    tables = (tile_values, tile_rows, tile_cols, tile_count, parity)
    table_specs = [VMEM, SMEM, SMEM, SMEM, SMEM]
    tile_flops = 2 * tile * tile * feat_cols
    wide = jax.ShapeDtypeStruct((feat_cols, node_count), jnp.float32)
    sent = jax.ShapeDtypeStruct((feat_cols, node_count), jnp.bfloat16)
    piece = jax.ShapeDtypeStruct((n_cols, feat_cols, width), jnp.bfloat16)
    total = pltpu.VMEM((feat_cols, node_count), jnp.float32)

    own = features.T
    even1 = even_swap(own)
    odd1 = odd_swap(own)
    weight_t = jnp.broadcast_to(weight.T, (n_cols, feat_cols, full))
    given = swapped(jnp.concatenate([pieces(cotangent.T), weight_t], 2))
    odd1, given = lax.optimization_barrier((odd1, given))
    odd2 = odd_swap(even1)
    even2 = even_swap(odd1)
    (near,) = call(
        near_kernel, tables + (own, even1, odd1), table_specs + [VMEM] * 3, [wide], flops=54 * tile_flops
    )
    (hidden,) = call(
        far_kernel,
        tables + (near, even2, odd2),
        table_specs + [VMEM] * 3,
        [piece],
        scratch=[total],
        flops=36 * tile_flops,
    )
    output, grads = call(
        dense_kernel,
        (swapped(hidden), given),
        [VMEM] * 2,
        [piece, jax.ShapeDtypeStruct((n_cols, feat_cols, width + full), jnp.bfloat16)],
        flops=6 * full * full * width,
    )
    grads = swapped(grads)
    even_far, odd_far = call(
        spread_far_kernel,
        tables + (grads,),
        table_specs + [VMEM],
        [sent, sent],
        scratch=[total, total],
        flops=36 * tile_flops,
    )
    even_in = even_swap(even_far)
    odd_in = odd_swap(odd_far)

    weight_grad = grads[:, :, width:].astype(jnp.float32).sum(0)
    weight_grad, even_far, odd_far = lax.optimization_barrier((weight_grad, even_far, odd_far))
    output = swapped(output)
    weight_grad = lax.all_gather(weight_grad, "zl").sum(0)
    even_in, odd_in, weight_grad = lax.optimization_barrier((even_in, odd_in, weight_grad))

    even_near, odd_near = call(
        spread_near_kernel,
        tables + (grads, odd_in, even_in),
        table_specs + [VMEM] * 3,
        [sent, sent],
        scratch=[total, total],
        flops=36 * tile_flops,
    )
    even_last = even_swap(even_near)
    odd_last = odd_swap(odd_near)
    weight_grad, even_near, odd_near = lax.optimization_barrier((weight_grad, even_near, odd_near))
    weight_grad = lax.all_gather(weight_grad, "zh").sum(0)
    weight_grad = weight_grad + lax.ppermute(weight_grad, "yh", swap_pairs(2, 0))
    (feature_grad,) = call(
        spread_own_kernel,
        tables + (grads, even_last, odd_last),
        table_specs + [VMEM] * 3,
        [sent],
        scratch=[total],
        flops=18 * tile_flops,
    )
    weight_grad, feature_grad = lax.optimization_barrier((weight_grad, feature_grad))
    weight_grad = lax.all_gather(weight_grad, "x").sum(0)
    weight_grad = (weight_grad * (1.0 / (node_count * n_rows) ** 0.5)).T
    output = output.transpose(1, 0, 2).reshape(feat_cols, node_count).T
    return (output, feature_grad.T, weight_grad)


def solution(mesh):
    n_rows, n_cols = mesh.shape["rows"], mesh.shape["cols"]
    devices = mesh.devices.reshape(2, n_rows // 32, 4, 4, 2, n_cols // 2)
    fine = Mesh(devices, ROWS + COLS)
    in_specs = (
        P(ROWS, COLS),
        P(None, COLS),
        P(ROWS, None, None),
        P(ROWS),
        P(ROWS),
        P(ROWS),
        P(ROWS, COLS),
    )
    out_specs = (P(ROWS, COLS), P(ROWS, COLS), P(None, COLS))
    return jax.shard_map(local, mesh=fine, in_specs=in_specs, out_specs=out_specs, check_vma=False)
```

```python
import jax
import jax.numpy as jnp
from jax import lax
from jax.experimental import pallas as pl
from jax.experimental.pallas import tpu as pltpu
from jax.sharding import Mesh, PartitionSpec as P

ROWS = ("yh", "z", "x")
COLS = ("yl", "core")
BLOCK = 128
NEAR = 5
VMEM = pl.BlockSpec(memory_space=pltpu.VMEM)
SMEM = pl.BlockSpec(memory_space=pltpu.SMEM)
BATCH = 6


def swap_pairs(count, odd):
    pairs = []
    for first in range(odd, count, 2):
        second = (first + 1) % count
        pairs += [(first, second), (second, first)]
    return pairs


def lanes(index):
    return pl.ds(pl.multiple_of(index * BLOCK, BLOCK), BLOCK)


def each_tile(offset, count, values_ref, term, add):
    slots = values_ref.shape[0]
    per_offset = -(-slots // NEAR)
    for first in range(0, per_offset, BATCH):
        held = []
        for k in range(first, min(first + BATCH, per_offset)):
            slot = k * NEAR + offset
            live = (slot < count).astype(jnp.float32)
            slot = jnp.minimum(slot, slots - 1)
            held.append((slot, term(slot) * live))
        for slot, product in held:
            add(slot, product)


def gather_terms(info, source_ref, total_ref, offset):
    values_ref, rows_ref, cols_ref, count = info
    blocks = source_ref.shape[1] // BLOCK

    def term(slot):
        source = source_ref[:, lanes(lax.rem(cols_ref[slot], blocks))]
        return lax.dot_general(
            source, values_ref[slot], (((1,), (1,)), ((), ())), preferred_element_type=jnp.float32
        )

    def add(slot, product):
        where = lanes(rows_ref[slot])
        total_ref[:, where] = total_ref[:, where] + product

    each_tile(offset, count, values_ref, term, add)


def near_kernel(values, rows, cols, count, parity, own, even, odd, total):
    total[...] = jnp.zeros_like(total)
    info = (values, rows, cols, count[0])
    even_offset = 3 - 2 * parity[0]
    gather_terms(info, own, total, 2)
    gather_terms(info, even, total, even_offset)
    gather_terms(info, odd, total, 4 - even_offset)


def far_kernel(values, rows, cols, count, parity, start, even, odd, hidden, total):
    total[...] = start[...]
    info = (values, rows, cols, count[0])
    even_offset = 4 - 4 * parity[0]
    gather_terms(info, even, total, even_offset)
    gather_terms(info, odd, total, 4 - even_offset)
    parts, _, width = hidden.shape
    for part in range(parts):
        hidden[part] = total[:, part * width : (part + 1) * width].astype(hidden.dtype)


def dense_kernel(hidden, grad_out, weight, output, sent):
    parts, cols, width = hidden.shape
    full = parts * cols
    source = hidden[...].reshape(full, width)
    weight_t = weight[...]
    preact = jnp.dot(weight_t, source, preferred_element_type=jnp.float32)
    sigmoid = 1.0 / (1.0 + jnp.exp(-preact))
    output[...] = (preact * sigmoid).astype(output.dtype).reshape(output.shape)
    slope = sigmoid * (1.0 + preact * (1.0 - sigmoid))
    grad = grad_out[...].reshape(full, width).astype(jnp.float32) * slope
    grad = grad.astype(jnp.bfloat16)
    back = lax.dot_general(
        weight_t, grad, (((0,), (0,)), ((), ())), preferred_element_type=jnp.float32
    )
    sent[:, :, :width] = back.astype(sent.dtype).reshape(parts, cols, width)
    weight_term = lax.dot_general(
        grad, source, (((1,), (1,)), ((), ())), preferred_element_type=jnp.float32
    )
    sent[:, :, width:] = weight_term.astype(sent.dtype).reshape(parts, cols, full)


def spread_terms(info, grad_ref, total_ref, offset):
    values_ref, rows_ref, cols_ref, count = info
    blocks = total_ref.shape[1] // BLOCK
    per_part = blocks // grad_ref.shape[0]

    def term(slot):
        row = rows_ref[slot]
        part = row // per_part
        source = grad_ref[part, :, lanes(row - part * per_part)]
        return jnp.dot(source, values_ref[slot], preferred_element_type=jnp.float32)

    def add(slot, product):
        where = lanes(lax.rem(cols_ref[slot], blocks))
        total_ref[:, where] = total_ref[:, where] + product

    each_tile(offset, count, values_ref, term, add)


def spread_far_kernel(values, rows, cols, count, parity, grad, even, odd, even_total, odd_total):
    info = (values, rows, cols, count[0])
    even_offset = 4 - 4 * parity[0]
    for offset, total, out in ((even_offset, even_total, even), (4 - even_offset, odd_total, odd)):
        total[...] = jnp.zeros_like(total)
        spread_terms(info, grad, total, offset)
        out[...] = total[...].astype(out.dtype)


def spread_near_kernel(
    values, rows, cols, count, parity, grad, from_odd, from_even, even, odd, even_total, odd_total
):
    info = (values, rows, cols, count[0])
    even_offset = 3 - 2 * parity[0]
    for offset, start, total, out in (
        (even_offset, from_odd, even_total, even),
        (4 - even_offset, from_even, odd_total, odd),
    ):
        total[...] = start[...].astype(total.dtype)
        spread_terms(info, grad, total, offset)
        out[...] = total[...].astype(out.dtype)


def spread_own_kernel(values, rows, cols, count, parity, grad, from_even, from_odd, out, total):
    info = (values, rows, cols, count[0])
    total[...] = from_even[...].astype(total.dtype) + from_odd[...].astype(total.dtype)
    spread_terms(info, grad, total, 2)
    out[...] = total[...].astype(out.dtype)


def call(kernel, args, specs, outs, scratch=(), flops=0):
    moved = sum(a.size * a.dtype.itemsize for a in args)
    moved += sum(o.size * o.dtype.itemsize for o in outs)
    return pl.pallas_call(
        kernel,
        out_shape=outs,
        in_specs=specs,
        out_specs=[VMEM] * len(outs),
        scratch_shapes=scratch,
        cost_estimate=pl.CostEstimate(flops=flops, bytes_accessed=moved, transcendentals=0),
        compiler_params=pltpu.CompilerParams(vmem_limit_bytes=24 << 20),
    )(*args)


def swapped(value):
    return lax.all_to_all(value, COLS, 0, 0, tiled=True)


def local(features, weight, tile_values, tile_rows, tile_cols, tile_count, cotangent):
    node_count, feat_cols = features.shape
    slots, tile, _ = tile_values.shape
    n_rows = lax.axis_size(ROWS)
    n_cols = lax.axis_size(COLS)
    width = node_count // n_cols
    full = feat_cols * n_cols
    even_pairs = swap_pairs(n_rows, 0)
    odd_pairs = swap_pairs(n_rows, 1)

    def even_swap(value):
        return lax.ppermute(value, ROWS, even_pairs)

    def odd_swap(value):
        return lax.ppermute(value, ROWS, odd_pairs)

    def pieces(value):
        return value.reshape(feat_cols, n_cols, width).transpose(1, 0, 2)

    parity = lax.rem(lax.axis_index("x"), 2).astype(jnp.int32).reshape(1)
    tables = (tile_values, tile_rows, tile_cols, tile_count, parity)
    table_specs = [VMEM, SMEM, SMEM, SMEM, SMEM]
    tile_flops = 2 * tile * tile * feat_cols
    wide = jax.ShapeDtypeStruct((feat_cols, node_count), jnp.float32)
    sent = jax.ShapeDtypeStruct((feat_cols, node_count), jnp.bfloat16)
    piece = jax.ShapeDtypeStruct((n_cols, feat_cols, width), jnp.bfloat16)
    total = pltpu.VMEM((feat_cols, node_count), jnp.float32)

    own = features.T
    even1 = even_swap(own)
    odd1 = odd_swap(own)
    grad_out = swapped(pieces(cotangent.T))
    odd1, grad_out = lax.optimization_barrier((odd1, grad_out))
    odd2 = odd_swap(even1)
    even2 = even_swap(odd1)
    weight_t, _ = lax.optimization_barrier((weight.T, grad_out))
    weight_t = lax.all_gather(weight_t, COLS, axis=0, tiled=True)
    own, weight_t = lax.optimization_barrier((own, weight_t))
    (near,) = call(
        near_kernel, tables + (own, even1, odd1), table_specs + [VMEM] * 3, [wide], flops=54 * tile_flops
    )
    (hidden,) = call(
        far_kernel,
        tables + (near, even2, odd2),
        table_specs + [VMEM] * 3,
        [piece],
        scratch=[total],
        flops=36 * tile_flops,
    )
    output, grads = call(
        dense_kernel,
        (swapped(hidden), grad_out, weight_t),
        [VMEM] * 3,
        [piece, jax.ShapeDtypeStruct((n_cols, feat_cols, width + full), jnp.bfloat16)],
        flops=6 * full * full * width,
    )
    grads = swapped(grads)
    even_far, odd_far = call(
        spread_far_kernel,
        tables + (grads,),
        table_specs + [VMEM],
        [sent, sent],
        scratch=[total, total],
        flops=36 * tile_flops,
    )
    even_in = even_swap(even_far)
    odd_in = odd_swap(odd_far)

    weight_grad = grads[:, :, width:].astype(jnp.float32).sum(0)
    weight_grad = lax.all_gather(weight_grad, "z")
    even_near, odd_near = call(
        spread_near_kernel,
        tables + (grads, odd_in, even_in),
        table_specs + [VMEM] * 3,
        [sent, sent],
        scratch=[total, total],
        flops=36 * tile_flops,
    )
    even_last = even_swap(even_near)
    odd_last = odd_swap(odd_near)
    output, even_near, odd_near = lax.optimization_barrier((output, even_near, odd_near))
    output = swapped(output)
    (feature_grad,) = call(
        spread_own_kernel,
        tables + (grads, even_last, odd_last),
        table_specs + [VMEM] * 3,
        [sent],
        scratch=[total],
        flops=18 * tile_flops,
    )
    weight_grad, feature_grad = lax.optimization_barrier((weight_grad, feature_grad))
    weight_grad = weight_grad.sum(0)
    weight_grad = weight_grad + lax.ppermute(weight_grad, "yh", swap_pairs(2, 0))
    weight_grad = lax.all_gather(weight_grad, "x").sum(0)
    weight_grad = (weight_grad * (1.0 / (node_count * n_rows) ** 0.5)).T
    output = output.transpose(1, 0, 2).reshape(feat_cols, node_count).T
    return (output, feature_grad.T, weight_grad)


def solution(mesh):
    n_rows, n_cols = mesh.shape["rows"], mesh.shape["cols"]
    devices = mesh.devices.reshape(2, n_rows // 8, 4, 2, n_cols // 2)
    fine = Mesh(devices, ROWS + COLS)
    in_specs = (
        P(ROWS, COLS),
        P(None, COLS),
        P(ROWS, None, None),
        P(ROWS),
        P(ROWS),
        P(ROWS),
        P(ROWS, COLS),
    )
    out_specs = (P(ROWS, COLS), P(ROWS, COLS), P(None, COLS))
    return jax.shard_map(local, mesh=fine, in_specs=in_specs, out_specs=out_specs, check_vma=False)
```

```python
import jax
import jax.numpy as jnp
from jax import lax
from jax.experimental import pallas as pl
from jax.experimental.pallas import tpu as pltpu
from jax.sharding import Mesh, PartitionSpec as P

ROWS = ("yh", "z", "x")
COLS = ("yl", "core")
BLOCK = 128
NEAR = 5
VMEM = pl.BlockSpec(memory_space=pltpu.VMEM)
SMEM = pl.BlockSpec(memory_space=pltpu.SMEM)
BATCH = 6


def swap_pairs(count, odd):
    pairs = []
    for first in range(odd, count, 2):
        second = (first + 1) % count
        pairs += [(first, second), (second, first)]
    return pairs


def lanes(index):
    return pl.ds(pl.multiple_of(index * BLOCK, BLOCK), BLOCK)


def wide_lanes(index, width):
    return pl.ds(pl.multiple_of(index * width, width), width)


def each_tile(offset, count, values_ref, term, add):
    slots = values_ref.shape[0]
    per_offset = -(-slots // NEAR)
    for first in range(0, per_offset, BATCH):
        held = []
        for k in range(first, min(first + BATCH, per_offset)):
            slot = k * NEAR + offset
            live = (slot < count).astype(jnp.float32)
            slot = jnp.minimum(slot, slots - 1)
            held.append((slot, term(slot) * live))
        for slot, product in held:
            add(slot, product)


def gather_terms(info, source_ref, total_ref, offset):
    values_ref, rows_ref, cols_ref, count = info
    blocks = source_ref.shape[1] // BLOCK

    def term(slot):
        source = source_ref[:, lanes(lax.rem(cols_ref[slot], blocks))]
        return lax.dot_general(
            source, values_ref[slot], (((1,), (1,)), ((), ())), preferred_element_type=jnp.float32
        )

    def add(slot, product):
        where = lanes(rows_ref[slot])
        total_ref[:, where] = total_ref[:, where] + product

    each_tile(offset, count, values_ref, term, add)


def near_kernel(values, rows, cols, count, place, own, even, odd, total):
    total[...] = jnp.zeros_like(total)
    info = (values, rows, cols, count[0])
    even_offset = 3 - 2 * place[0]
    gather_terms(info, own, total, 2)
    gather_terms(info, even, total, even_offset)
    gather_terms(info, odd, total, 4 - even_offset)


def pack_kernel(place, cotangent, weight, *packed):
    width = packed[0].shape[1] - weight.shape[1]
    for step, out in enumerate(packed):
        out[:, :width] = cotangent[:, wide_lanes(place[1] ^ step, width)]
        out[:, width:] = weight[...]


def far_kernel(values, rows, cols, count, place, start, even, odd, *rest):
    hidden, total = rest[:-1], rest[-1]
    total[...] = start[...]
    info = (values, rows, cols, count[0])
    even_offset = 4 - 4 * place[0]
    gather_terms(info, even, total, even_offset)
    gather_terms(info, odd, total, 4 - even_offset)
    for step, out in enumerate(hidden):
        width = out.shape[1]
        out[...] = total[:, wide_lanes(place[1] ^ step, width)].astype(out.dtype)


def dense_kernel(place, *refs):
    n = (len(refs) - 2) // 4
    hidden, given, output, sent = (refs[k * n : (k + 1) * n] for k in range(4))
    source_ref, back_ref = refs[4 * n :]
    cols, width = hidden[0].shape

    def group(step):
        return pl.ds(pl.multiple_of((place[1] ^ step) * cols, cols), cols)

    for step in range(n):
        source_ref[group(step), :] = hidden[step][...]
    source = source_ref[...]
    weight_t = jnp.concatenate([ref[:, width:] for ref in given], 0)
    preact = jnp.dot(weight_t, source, preferred_element_type=jnp.float32)
    sigmoid = 1.0 / (1.0 + jnp.exp(-preact))
    value = (preact * sigmoid).astype(jnp.bfloat16)
    slope = sigmoid * (1.0 + preact * (1.0 - sigmoid))
    grad = jnp.concatenate([ref[:, :width] for ref in given], 0).astype(jnp.float32) * slope
    grad = grad.astype(jnp.bfloat16)
    back = lax.dot_general(
        weight_t, grad, (((0,), (0,)), ((), ())), preferred_element_type=jnp.float32
    )
    back_ref[...] = back.astype(back_ref.dtype)
    weight_term = lax.dot_general(
        grad, source, (((1,), (1,)), ((), ())), preferred_element_type=jnp.float32
    ).astype(jnp.bfloat16)
    for step in range(n):
        here = slice(step * cols, (step + 1) * cols)
        output[step][...] = value[here]
        sent[step][:, :width] = back_ref[group(step), :]
        sent[step][:, width:] = weight_term[here]


def spread_terms(info, grad_ref, total_ref, offset):
    values_ref, rows_ref, cols_ref, count = info
    blocks = total_ref.shape[1] // BLOCK
    per_part = blocks // grad_ref.shape[0]

    def term(slot):
        row = rows_ref[slot]
        part = row // per_part
        source = grad_ref[part, :, lanes(row - part * per_part)]
        return jnp.dot(source, values_ref[slot], preferred_element_type=jnp.float32)

    def add(slot, product):
        where = lanes(lax.rem(cols_ref[slot], blocks))
        total_ref[:, where] = total_ref[:, where] + product

    each_tile(offset, count, values_ref, term, add)


def spread_far_kernel(values, rows, cols, count, place, *refs):
    n = len(refs) - 6
    sent = refs[:n]
    even, odd, grads, weight_sum, even_total, odd_total = refs[n:]
    width = grads.shape[2]
    for step, ref in enumerate(sent):
        grads[place[1] ^ step] = ref[:, :width]
    info = (values, rows, cols, count[0])
    even_offset = 4 - 4 * place[0]
    for offset, total, out in ((even_offset, even_total, even), (4 - even_offset, odd_total, odd)):
        total[...] = jnp.zeros_like(total)
        spread_terms(info, grads, total, offset)
        out[...] = total[...].astype(out.dtype)
    terms = [ref[:, width:].astype(jnp.float32) for ref in sent]
    weight_sum[...] = sum(terms[1:], terms[0])


def spread_near_kernel(
    values, rows, cols, count, place, grad, from_odd, from_even, even, odd, even_total, odd_total
):
    info = (values, rows, cols, count[0])
    even_offset = 3 - 2 * place[0]
    for offset, start, total, out in (
        (even_offset, from_odd, even_total, even),
        (4 - even_offset, from_even, odd_total, odd),
    ):
        total[...] = start[...].astype(total.dtype)
        spread_terms(info, grad, total, offset)
        out[...] = total[...].astype(out.dtype)


def spread_own_kernel(values, rows, cols, count, place, grad, from_even, from_odd, *refs):
    parts, (out, output, total) = refs[:-3], refs[-3:]
    info = (values, rows, cols, count[0])
    total[...] = from_even[...].astype(total.dtype) + from_odd[...].astype(total.dtype)
    spread_terms(info, grad, total, 2)
    out[...] = total[...].astype(out.dtype)
    for step, part in enumerate(parts):
        output[:, wide_lanes(place[1] ^ step, part.shape[1])] = part[...]


def call(kernel, args, specs, outs, scratch=(), flops=0):
    moved = sum(a.size * a.dtype.itemsize for a in args)
    moved += sum(o.size * o.dtype.itemsize for o in outs)
    return pl.pallas_call(
        kernel,
        out_shape=outs,
        in_specs=specs,
        out_specs=[VMEM] * len(outs),
        scratch_shapes=scratch,
        cost_estimate=pl.CostEstimate(flops=flops, bytes_accessed=moved, transcendentals=0),
        compiler_params=pltpu.CompilerParams(vmem_limit_bytes=24 << 20),
    )(*args)


def swapped(values):
    def pairs(step):
        return [(source, source ^ step) for source in range(len(values))]

    return [values[0]] + [
        lax.ppermute(value, COLS, pairs(step)) for step, value in enumerate(values) if step
    ]


def doubled(value, axis, step):
    count = lax.axis_size(axis)
    return value + lax.ppermute(value, axis, [(source, source ^ step) for source in range(count)])


def local(features, weight, tile_values, tile_rows, tile_cols, tile_count, cotangent):
    node_count, feat_cols = features.shape
    slots, tile, _ = tile_values.shape
    n_rows = lax.axis_size(ROWS)
    n_cols = lax.axis_size(COLS)
    width = node_count // n_cols
    full = feat_cols * n_cols
    even_pairs = swap_pairs(n_rows, 0)
    odd_pairs = swap_pairs(n_rows, 1)

    def even_swap(value):
        return lax.ppermute(value, ROWS, even_pairs)

    def odd_swap(value):
        return lax.ppermute(value, ROWS, odd_pairs)

    place = jnp.stack([lax.rem(lax.axis_index("x"), 2), lax.axis_index(COLS)]).astype(jnp.int32)
    tables = (tile_values, tile_rows, tile_cols, tile_count, place)
    table_specs = [VMEM, SMEM, SMEM, SMEM, SMEM]
    tile_flops = 2 * tile * tile * feat_cols

    def arrays(number, shape, dtype=jnp.bfloat16):
        return [jax.ShapeDtypeStruct(shape, dtype)] * number

    whole = (feat_cols, node_count)
    total = pltpu.VMEM(whole, jnp.float32)

    own = features.T
    even1 = even_swap(own)
    odd1 = odd_swap(own)
    given = call(
        pack_kernel,
        (place, cotangent.T, weight.T),
        [SMEM, VMEM, VMEM],
        arrays(n_cols, (feat_cols, width + full)),
    )
    even1, _ = lax.optimization_barrier((even1, given[0]))
    given = swapped(given)
    odd2 = odd_swap(even1)
    even2 = even_swap(odd1)
    (near,) = call(
        near_kernel,
        tables + (own, even1, odd1),
        table_specs + [VMEM] * 3,
        arrays(1, whole, jnp.float32),
        flops=54 * tile_flops,
    )
    hidden = call(
        far_kernel,
        tables + (near, even2, odd2),
        table_specs + [VMEM] * 3,
        arrays(n_cols, (feat_cols, width)),
        scratch=[total],
        flops=36 * tile_flops,
    )
    both = call(
        dense_kernel,
        (place, *swapped(hidden), *given),
        [SMEM] + [VMEM] * (2 * n_cols),
        arrays(n_cols, (feat_cols, width)) + arrays(n_cols, (feat_cols, width + full)),
        scratch=[pltpu.VMEM((full, width), jnp.bfloat16)] * 2,
        flops=6 * full * full * width,
    )
    output, sent = list(both[:n_cols]), swapped(both[n_cols:])
    even_far, odd_far, grads, weight_grad = call(
        spread_far_kernel,
        tables + tuple(sent),
        table_specs + [VMEM] * n_cols,
        arrays(2, whole) + arrays(1, (n_cols, feat_cols, width)) + arrays(1, (feat_cols, full), jnp.float32),
        scratch=[total, total],
        flops=36 * tile_flops,
    )
    even_in = even_swap(even_far)
    odd_in = odd_swap(odd_far)
    weight_grad = doubled(doubled(weight_grad, "z", 1), "z", 2)
    even_in, odd_in, weight_grad = lax.optimization_barrier((even_in, odd_in, weight_grad))
    even_near, odd_near = call(
        spread_near_kernel,
        tables + (grads, odd_in, even_in),
        table_specs + [VMEM] * 3,
        arrays(2, whole),
        scratch=[total, total],
        flops=36 * tile_flops,
    )
    even_last = even_swap(even_near)
    odd_last = odd_swap(odd_near)
    output[0], even_near = lax.optimization_barrier((output[0], even_near))
    output = swapped(output)
    weight_grad = doubled(weight_grad, "z", 4)
    feature_grad, output = call(
        spread_own_kernel,
        tables + (grads, even_last, odd_last, *output),
        table_specs + [VMEM] * (3 + n_cols),
        arrays(2, whole),
        scratch=[total],
        flops=18 * tile_flops,
    )
    weight_grad = doubled(weight_grad, "z", 8)
    weight_grad = doubled(weight_grad, "yh", 1)
    weight_grad = lax.all_gather(weight_grad, "x").sum(0)
    weight_grad = (weight_grad * (1.0 / (node_count * n_rows) ** 0.5)).T
    return (output.T, feature_grad.T, weight_grad)


def solution(mesh):
    n_rows, n_cols = mesh.shape["rows"], mesh.shape["cols"]
    devices = mesh.devices.reshape(2, n_rows // 8, 4, 2, n_cols // 2)
    fine = Mesh(devices, ROWS + COLS)
    in_specs = (
        P(ROWS, COLS),
        P(None, COLS),
        P(ROWS, None, None),
        P(ROWS),
        P(ROWS),
        P(ROWS),
        P(ROWS, COLS),
    )
    out_specs = (P(ROWS, COLS), P(ROWS, COLS), P(None, COLS))
    return jax.shard_map(local, mesh=fine, in_specs=in_specs, out_specs=out_specs, check_vma=False)
```

```python
import functools

import jax
import jax.numpy as jnp
from jax import lax
from jax.experimental import pallas as pl
from jax.experimental.pallas import tpu as pltpu
from jax.sharding import Mesh, PartitionSpec as P

ROWS = ("yh", "z", "x")
COLS = ("yl", "core")
BLOCK = 128
NEAR = 5
VMEM = pl.BlockSpec(memory_space=pltpu.VMEM)
SMEM = pl.BlockSpec(memory_space=pltpu.SMEM)
BATCH = 6


def swap_pairs(count, odd):
    pairs = []
    for first in range(odd, count, 2):
        second = (first + 1) % count
        pairs += [(first, second), (second, first)]
    return pairs


def lanes(index):
    return pl.ds(pl.multiple_of(index * BLOCK, BLOCK), BLOCK)


def wide_lanes(index, width):
    return pl.ds(pl.multiple_of(index * width, width), width)


def each_tile(offset, count, values_ref, term, add):
    slots = values_ref.shape[0]
    per_offset = -(-slots // NEAR)
    for first in range(0, per_offset, BATCH):
        held = []
        for k in range(first, min(first + BATCH, per_offset)):
            slot = k * NEAR + offset
            live = (slot < count).astype(jnp.float32)
            slot = jnp.minimum(slot, slots - 1)
            held.append((slot, term(slot) * live))
        for slot, product in held:
            add(slot, product)


def gather_terms(info, source_ref, total_ref, offset):
    values_ref, rows_ref, cols_ref, count = info
    blocks = source_ref.shape[1] // BLOCK

    def term(slot):
        source = source_ref[:, lanes(lax.rem(cols_ref[slot], blocks))]
        return lax.dot_general(
            source, values_ref[slot], (((1,), (1,)), ((), ())), preferred_element_type=jnp.float32
        )

    def add(slot, product):
        where = lanes(rows_ref[slot])
        total_ref[:, where] = total_ref[:, where] + product

    each_tile(offset, count, values_ref, term, add)


def first_kernel(values, rows, cols, count, place, own, even, total):
    total[...] = jnp.zeros_like(total)
    info = (values, rows, cols, count[0])
    gather_terms(info, own, total, 2)
    gather_terms(info, even, total, 3 - 2 * place[0])


def second_kernel(values, rows, cols, count, place, start, odd, total):
    total[...] = start[...]
    gather_terms((values, rows, cols, count[0]), odd, total, 1 + 2 * place[0])


def pack_kernel(place, cotangent, weight, *packed):
    width = packed[0].shape[1] - weight.shape[1]
    for step, out in enumerate(packed):
        out[:, :width] = cotangent[:, wide_lanes(place[1] ^ step, width)]
        out[:, width:] = weight[...]


def far_kernel(values, rows, cols, count, place, start, even, odd, *rest):
    hidden, total = rest[:-1], rest[-1]
    total[...] = start[...]
    info = (values, rows, cols, count[0])
    even_offset = 4 - 4 * place[0]
    gather_terms(info, even, total, even_offset)
    gather_terms(info, odd, total, 4 - even_offset)
    for step, out in enumerate(hidden):
        width = out.shape[1]
        out[...] = total[:, wide_lanes(place[1] ^ step, width)].astype(out.dtype)


def dense_kernel(place, *refs):
    n = (len(refs) - 2) // 4
    hidden, given, output, sent = (refs[k * n : (k + 1) * n] for k in range(4))
    source_ref, back_ref = refs[4 * n :]
    cols, width = hidden[0].shape

    def group(step):
        return pl.ds(pl.multiple_of((place[1] ^ step) * cols, cols), cols)

    for step in range(n):
        source_ref[group(step), :] = hidden[step][...]
    source = source_ref[...]
    weight_t = jnp.concatenate([ref[:, width:] for ref in given], 0)
    preact = jnp.dot(weight_t, source, preferred_element_type=jnp.float32)
    sigmoid = 1.0 / (1.0 + jnp.exp(-preact))
    value = (preact * sigmoid).astype(jnp.bfloat16)
    slope = sigmoid * (1.0 + preact * (1.0 - sigmoid))
    grad = jnp.concatenate([ref[:, :width] for ref in given], 0).astype(jnp.float32) * slope
    grad = grad.astype(jnp.bfloat16)
    back = lax.dot_general(
        weight_t, grad, (((0,), (0,)), ((), ())), preferred_element_type=jnp.float32
    )
    back_ref[...] = back.astype(back_ref.dtype)
    weight_term = lax.dot_general(
        grad, source, (((1,), (1,)), ((), ())), preferred_element_type=jnp.float32
    ).astype(jnp.bfloat16)
    for step in range(n):
        here = slice(step * cols, (step + 1) * cols)
        output[step][...] = value[here]
        sent[step][:, :width] = back_ref[group(step), :]
        sent[step][:, width:] = weight_term[here]


def spread_terms(info, grad_ref, total_ref, offset):
    values_ref, rows_ref, cols_ref, count = info
    blocks = total_ref.shape[1] // BLOCK
    per_part = blocks // grad_ref.shape[0]

    def term(slot):
        row = rows_ref[slot]
        part = row // per_part
        source = grad_ref[part, :, lanes(row - part * per_part)]
        return jnp.dot(source, values_ref[slot], preferred_element_type=jnp.float32)

    def add(slot, product):
        where = lanes(lax.rem(cols_ref[slot], blocks))
        total_ref[:, where] = total_ref[:, where] + product

    each_tile(offset, count, values_ref, term, add)


def spread_far_kernel(values, rows, cols, count, place, *refs):
    n = len(refs) - 5
    sent = refs[:n]
    even, odd, grads, even_total, odd_total = refs[n:]
    width = grads.shape[2]
    for step, ref in enumerate(sent):
        grads[place[1] ^ step] = ref[:, :width]
    info = (values, rows, cols, count[0])
    even_offset = 4 - 4 * place[0]
    for offset, total, out in ((even_offset, even_total, even), (4 - even_offset, odd_total, odd)):
        total[...] = jnp.zeros_like(total)
        spread_terms(info, grads, total, offset)
        out[...] = total[...].astype(out.dtype)


def spread_near_kernel(offset, sign, values, rows, cols, count, place, grad, received, out, total):
    total[...] = received[...].astype(total.dtype)
    spread_terms((values, rows, cols, count[0]), grad, total, offset + sign * place[0])
    out[...] = total[...].astype(out.dtype)


def spread_own_kernel(values, rows, cols, count, place, grad, from_even, from_odd, *refs):
    parts, (out, output, total) = refs[:-3], refs[-3:]
    info = (values, rows, cols, count[0])
    total[...] = from_even[...].astype(total.dtype) + from_odd[...].astype(total.dtype)
    spread_terms(info, grad, total, 2)
    out[...] = total[...].astype(out.dtype)
    for step, part in enumerate(parts):
        output[:, wide_lanes(place[1] ^ step, part.shape[1])] = part[...]


def call(kernel, args, specs, outs, scratch=(), flops=0):
    moved = sum(a.size * a.dtype.itemsize for a in args)
    moved += sum(o.size * o.dtype.itemsize for o in outs)
    return pl.pallas_call(
        kernel,
        out_shape=outs,
        in_specs=specs,
        out_specs=[VMEM] * len(outs),
        scratch_shapes=scratch,
        cost_estimate=pl.CostEstimate(flops=flops, bytes_accessed=moved, transcendentals=0),
        compiler_params=pltpu.CompilerParams(vmem_limit_bytes=24 << 20),
    )(*args)


def swapped(values):
    def pairs(step):
        return [(source, source ^ step) for source in range(len(values))]

    moved = list(values)
    for step in reversed(range(1, len(values))):
        moved[step] = lax.ppermute(values[step], COLS, pairs(step))
    return moved


def doubled(value, axis, step):
    count = lax.axis_size(axis)
    return value + lax.ppermute(value, axis, [(source, source ^ step) for source in range(count)])


def local(features, weight, tile_values, tile_rows, tile_cols, tile_count, cotangent):
    node_count, feat_cols = features.shape
    slots, tile, _ = tile_values.shape
    n_rows = lax.axis_size(ROWS)
    n_cols = lax.axis_size(COLS)
    width = node_count // n_cols
    full = feat_cols * n_cols
    even_pairs = swap_pairs(n_rows, 0)
    odd_pairs = swap_pairs(n_rows, 1)

    def even_swap(value):
        return lax.ppermute(value, ROWS, even_pairs)

    def odd_swap(value):
        return lax.ppermute(value, ROWS, odd_pairs)

    place = jnp.stack([lax.rem(lax.axis_index("x"), 2), lax.axis_index(COLS)]).astype(jnp.int32)
    tables = (tile_values, tile_rows, tile_cols, tile_count, place)
    table_specs = [VMEM, SMEM, SMEM, SMEM, SMEM]
    tile_flops = 2 * tile * tile * feat_cols

    def arrays(number, shape, dtype=jnp.bfloat16):
        return [jax.ShapeDtypeStruct(shape, dtype)] * number

    whole = (feat_cols, node_count)
    total = pltpu.VMEM(whole, jnp.float32)

    own = features.T
    even1 = even_swap(own)
    odd1 = odd_swap(own)
    given = call(
        pack_kernel,
        (place, cotangent.T, weight.T),
        [SMEM, VMEM, VMEM],
        arrays(n_cols, (feat_cols, width + full)),
    )
    even1, _ = lax.optimization_barrier((even1, given[0]))
    given = swapped(given)
    odd2 = odd_swap(even1)
    (first,) = call(
        first_kernel,
        tables + (own, even1),
        table_specs + [VMEM] * 2,
        arrays(1, whole, jnp.float32),
        flops=36 * tile_flops,
    )
    odd1, first = lax.optimization_barrier((odd1, first))
    even2 = even_swap(odd1)
    (near,) = call(
        second_kernel,
        tables + (first, odd1),
        table_specs + [VMEM] * 2,
        arrays(1, whole, jnp.float32),
        flops=18 * tile_flops,
    )
    hidden = call(
        far_kernel,
        tables + (near, even2, odd2),
        table_specs + [VMEM] * 3,
        arrays(n_cols, (feat_cols, width)),
        scratch=[total],
        flops=36 * tile_flops,
    )
    both = call(
        dense_kernel,
        (place, *swapped(hidden), *given),
        [SMEM] + [VMEM] * (2 * n_cols),
        arrays(n_cols, (feat_cols, width)) + arrays(n_cols, (feat_cols, width + full)),
        scratch=[pltpu.VMEM((full, width), jnp.bfloat16)] * 2,
        flops=6 * full * full * width,
    )
    output, sent = list(both[:n_cols]), swapped(both[n_cols:])
    terms = [value[:, width:].astype(jnp.float32) for value in sent]
    weight_grad = doubled(sum(terms[1:], terms[0]), "z", 1)
    even_far, odd_far, grads = call(
        spread_far_kernel,
        tables + tuple(sent),
        table_specs + [VMEM] * n_cols,
        arrays(2, whole) + arrays(1, (n_cols, feat_cols, width)),
        scratch=[total, total],
        flops=36 * tile_flops,
    )
    even_in = even_swap(even_far)
    odd_in = odd_swap(odd_far)
    weight_grad = doubled(doubled(weight_grad, "yh", 1), "z", 2)

    def near_terms(offset, sign, received):
        return call(
            functools.partial(spread_near_kernel, offset, sign),
            tables + (grads, received),
            table_specs + [VMEM] * 2,
            arrays(1, whole),
            scratch=[total],
            flops=18 * tile_flops,
        )[0]

    even_in, _ = lax.optimization_barrier((even_in, weight_grad))
    odd_near = near_terms(1, 2, even_in)
    odd_last = odd_swap(odd_near)
    odd_in, _ = lax.optimization_barrier((odd_in, odd_near))
    even_near = near_terms(3, -2, odd_in)
    even_last = even_swap(even_near)
    far = lax.ppermute(weight_grad, "z", [(source, source ^ 4) for source in range(n_rows // 8)])
    far, _, output[0] = lax.optimization_barrier((far, even_near, output[0]))
    weight_grad = weight_grad + far
    weight_grad = doubled(weight_grad, "z", 8)
    output = swapped(output)
    feature_grad, output = call(
        spread_own_kernel,
        tables + (grads, even_last, odd_last, *output),
        table_specs + [VMEM] * (3 + n_cols),
        arrays(2, whole),
        scratch=[total],
        flops=18 * tile_flops,
    )
    weight_grad = lax.all_gather(weight_grad, "x").sum(0)
    weight_grad = (weight_grad * (1.0 / (node_count * n_rows) ** 0.5)).T
    return (output.T, feature_grad.T, weight_grad)


def solution(mesh):
    n_rows, n_cols = mesh.shape["rows"], mesh.shape["cols"]
    devices = mesh.devices.reshape(2, n_rows // 8, 4, 2, n_cols // 2)
    fine = Mesh(devices, ROWS + COLS)
    in_specs = (
        P(ROWS, COLS),
        P(None, COLS),
        P(ROWS, None, None),
        P(ROWS),
        P(ROWS),
        P(ROWS),
        P(ROWS, COLS),
    )
    out_specs = (P(ROWS, COLS), P(ROWS, COLS), P(None, COLS))
    return jax.shard_map(local, mesh=fine, in_specs=in_specs, out_specs=out_specs, check_vma=False)
```

```python
import functools

import jax
import jax.numpy as jnp
from jax import lax
from jax.experimental import pallas as pl
from jax.experimental.pallas import tpu as pltpu
from jax.sharding import Mesh, PartitionSpec as P

ROWS = ("yh", "z", "x")
COLS = ("yl", "core")
BLOCK = 128
NEAR = 5
VMEM = pl.BlockSpec(memory_space=pltpu.VMEM)
SMEM = pl.BlockSpec(memory_space=pltpu.SMEM)
BATCH = 6
PARTNERS = (0, 3, 2, 1)


def swap_pairs(count, odd):
    pairs = []
    for first in range(odd, count, 2):
        second = (first + 1) % count
        pairs += [(first, second), (second, first)]
    return pairs


def lanes(index):
    return pl.ds(pl.multiple_of(index * BLOCK, BLOCK), BLOCK)


def wide_lanes(index, width):
    return pl.ds(pl.multiple_of(index * width, width), width)


def each_tile(offset, count, values_ref, term, add):
    slots = values_ref.shape[0]
    per_offset = -(-slots // NEAR)
    for first in range(0, per_offset, BATCH):
        held = []
        for k in range(first, min(first + BATCH, per_offset)):
            slot = k * NEAR + offset
            live = (slot < count).astype(jnp.float32)
            slot = jnp.minimum(slot, slots - 1)
            held.append((slot, term(slot) * live))
        for slot, product in held:
            add(slot, product)


def gather_terms(info, source_ref, total_ref, offset):
    values_ref, rows_ref, cols_ref, count = info
    blocks = source_ref.shape[1] // BLOCK

    def term(slot):
        source = source_ref[:, lanes(lax.rem(cols_ref[slot], blocks))]
        return lax.dot_general(
            source, values_ref[slot], (((1,), (1,)), ((), ())), preferred_element_type=jnp.float32
        )

    def add(slot, product):
        where = lanes(rows_ref[slot])
        total_ref[:, where] = total_ref[:, where] + product

    each_tile(offset, count, values_ref, term, add)


def first_kernel(values, rows, cols, count, place, own, even, total):
    total[...] = jnp.zeros_like(total)
    info = (values, rows, cols, count[0])
    gather_terms(info, own, total, 2)
    gather_terms(info, even, total, 3 - 2 * place[0])


def second_kernel(values, rows, cols, count, place, start, odd, total):
    total[...] = start[...]
    gather_terms((values, rows, cols, count[0]), odd, total, 1 + 2 * place[0])


def pack_kernel(place, cotangent, weight, *packed):
    width = packed[0].shape[1] - weight.shape[1]
    for step, out in enumerate(packed):
        out[:, :width] = cotangent[:, wide_lanes(place[1] ^ PARTNERS[step], width)]
        out[:, width:] = weight[...]


def far_kernel(values, rows, cols, count, place, start, even, odd, *rest):
    hidden, total = rest[:-1], rest[-1]
    total[...] = start[...]
    info = (values, rows, cols, count[0])
    even_offset = 4 - 4 * place[0]
    gather_terms(info, even, total, even_offset)
    gather_terms(info, odd, total, 4 - even_offset)
    for step, out in enumerate(hidden):
        width = out.shape[1]
        out[...] = total[:, wide_lanes(place[1] ^ PARTNERS[step], width)].astype(out.dtype)


def dense_kernel(place, *refs):
    n = (len(refs) - 2) // 4
    hidden, given, sent, output = (refs[k * n : (k + 1) * n] for k in range(4))
    source_ref, back_ref = refs[4 * n :]
    cols, width = hidden[0].shape

    def group(step):
        return pl.ds(pl.multiple_of((place[1] ^ PARTNERS[step]) * cols, cols), cols)

    for step in range(n):
        source_ref[group(step), :] = hidden[step][...]
    source = source_ref[...]
    weight_t = jnp.concatenate([ref[:, width:] for ref in given], 0)
    preact = jnp.dot(weight_t, source, preferred_element_type=jnp.float32)
    sigmoid = 1.0 / (1.0 + jnp.exp(-preact))
    value = (preact * sigmoid).astype(jnp.bfloat16)
    slope = sigmoid * (1.0 + preact * (1.0 - sigmoid))
    grad = jnp.concatenate([ref[:, :width] for ref in given], 0).astype(jnp.float32) * slope
    grad = grad.astype(jnp.bfloat16)
    back = lax.dot_general(
        weight_t, grad, (((0,), (0,)), ((), ())), preferred_element_type=jnp.float32
    )
    back_ref[...] = back.astype(back_ref.dtype)
    weight_term = lax.dot_general(
        grad, source, (((1,), (1,)), ((), ())), preferred_element_type=jnp.float32
    ).astype(jnp.bfloat16)
    for step in range(n):
        here = slice(step * cols, (step + 1) * cols)
        output[step][...] = value[here]
        sent[step][:, :width] = back_ref[group(step), :]
        sent[step][:, width:] = weight_term[here]


def spread_terms(info, grad_ref, total_ref, offset):
    values_ref, rows_ref, cols_ref, count = info
    blocks = total_ref.shape[1] // BLOCK
    per_part = blocks // grad_ref.shape[0]

    def term(slot):
        row = rows_ref[slot]
        part = row // per_part
        source = grad_ref[part, :, lanes(row - part * per_part)]
        return jnp.dot(source, values_ref[slot], preferred_element_type=jnp.float32)

    def add(slot, product):
        where = lanes(lax.rem(cols_ref[slot], blocks))
        total_ref[:, where] = total_ref[:, where] + product

    each_tile(offset, count, values_ref, term, add)


def spread_far_kernel(values, rows, cols, count, place, *refs):
    n = len(refs) - 5
    sent = refs[:n]
    even, odd, grads, even_total, odd_total = refs[n:]
    width = grads.shape[2]
    for step, ref in enumerate(sent):
        grads[place[1] ^ PARTNERS[step]] = ref[:, :width]
    info = (values, rows, cols, count[0])
    even_offset = 4 - 4 * place[0]
    for offset, total, out in ((even_offset, even_total, even), (4 - even_offset, odd_total, odd)):
        total[...] = jnp.zeros_like(total)
        spread_terms(info, grads, total, offset)
        out[...] = total[...].astype(out.dtype)


def spread_near_kernel(offset, sign, values, rows, cols, count, place, grad, received, out, total):
    total[...] = received[...].astype(total.dtype)
    spread_terms((values, rows, cols, count[0]), grad, total, offset + sign * place[0])
    out[...] = total[...].astype(out.dtype)


def spread_own_kernel(values, rows, cols, count, place, grad, from_even, from_odd, *refs):
    parts, (out, output, total) = refs[:-3], refs[-3:]
    info = (values, rows, cols, count[0])
    total[...] = from_even[...].astype(total.dtype) + from_odd[...].astype(total.dtype)
    spread_terms(info, grad, total, 2)
    out[...] = total[...].astype(out.dtype)
    for step, part in enumerate(parts):
        output[:, wide_lanes(place[1] ^ PARTNERS[step], part.shape[1])] = part[...]


def call(kernel, args, specs, outs, scratch=(), flops=0):
    moved = sum(a.size * a.dtype.itemsize for a in args)
    moved += sum(o.size * o.dtype.itemsize for o in outs)
    return pl.pallas_call(
        kernel,
        out_shape=outs,
        in_specs=specs,
        out_specs=[VMEM] * len(outs),
        scratch_shapes=scratch,
        cost_estimate=pl.CostEstimate(flops=flops, bytes_accessed=moved, transcendentals=0),
        compiler_params=pltpu.CompilerParams(vmem_limit_bytes=24 << 20),
    )(*args)


def swapped(values):
    def pairs(step):
        return [(source, source ^ PARTNERS[step]) for source in range(len(values))]

    return [values[0]] + [
        lax.ppermute(value, COLS, pairs(step)) for step, value in enumerate(values) if step
    ]


def summed(value, axis):
    copies = jnp.broadcast_to(value, (lax.axis_size(axis), *value.shape))
    return lax.all_to_all(copies, axis, 0, 0, tiled=True).sum(0)


def paired(value, axis, step):
    count = lax.axis_size(axis)
    return lax.ppermute(value, axis, [(source, source ^ step) for source in range(count)])


def local(features, weight, tile_values, tile_rows, tile_cols, tile_count, cotangent):
    node_count, feat_cols = features.shape
    slots, tile, _ = tile_values.shape
    n_rows = lax.axis_size(ROWS)
    n_cols = lax.axis_size(COLS)
    width = node_count // n_cols
    full = feat_cols * n_cols
    even_pairs = swap_pairs(n_rows, 0)
    odd_pairs = swap_pairs(n_rows, 1)

    def even_swap(value):
        return lax.ppermute(value, ROWS, even_pairs)

    def odd_swap(value):
        return lax.ppermute(value, ROWS, odd_pairs)

    place = jnp.stack([lax.rem(lax.axis_index("x"), 2), lax.axis_index(COLS)]).astype(jnp.int32)
    tables = (tile_values, tile_rows, tile_cols, tile_count, place)
    table_specs = [VMEM, SMEM, SMEM, SMEM, SMEM]
    tile_flops = 2 * tile * tile * feat_cols

    def arrays(number, shape, dtype=jnp.bfloat16):
        return [jax.ShapeDtypeStruct(shape, dtype)] * number

    whole = (feat_cols, node_count)
    total = pltpu.VMEM(whole, jnp.float32)

    own = features.T
    even1 = even_swap(own)
    odd1 = odd_swap(own)
    given = call(
        pack_kernel,
        (place, cotangent.T, weight.T),
        [SMEM, VMEM, VMEM],
        arrays(n_cols, (feat_cols, width + full)),
    )
    even1, _ = lax.optimization_barrier((even1, given[0]))
    given = swapped(given)
    odd2 = odd_swap(even1)
    (first,) = call(
        first_kernel,
        tables + (own, even1),
        table_specs + [VMEM] * 2,
        arrays(1, whole, jnp.float32),
        flops=36 * tile_flops,
    )
    odd1, first = lax.optimization_barrier((odd1, first))
    even2 = even_swap(odd1)
    (near,) = call(
        second_kernel,
        tables + (first, odd1),
        table_specs + [VMEM] * 2,
        arrays(1, whole, jnp.float32),
        flops=18 * tile_flops,
    )
    hidden = call(
        far_kernel,
        tables + (near, even2, odd2),
        table_specs + [VMEM] * 3,
        arrays(n_cols, (feat_cols, width)),
        scratch=[total],
        flops=36 * tile_flops,
    )
    both = call(
        dense_kernel,
        (place, *swapped(hidden), *given),
        [SMEM] + [VMEM] * (2 * n_cols),
        arrays(n_cols, (feat_cols, width + full)) + arrays(n_cols, (feat_cols, width)),
        scratch=[pltpu.VMEM((full, width), jnp.bfloat16)] * 2,
        flops=6 * full * full * width,
    )
    output, sent = both[n_cols:], swapped(both[:n_cols])
    terms = [value[:, width:].astype(jnp.float32) for value in sent]
    weight_grad = sum(terms[1:], terms[0])
    even_far, odd_far, grads = call(
        spread_far_kernel,
        tables + tuple(sent),
        table_specs + [VMEM] * n_cols,
        arrays(2, whole) + arrays(1, (n_cols, feat_cols, width)),
        scratch=[total, total],
        flops=36 * tile_flops,
    )
    even_in = even_swap(even_far)
    odd_in = odd_swap(odd_far)
    weight_grad, _ = lax.optimization_barrier((weight_grad, even_far))
    weight_grad = weight_grad + paired(weight_grad, "z", 1)
    weight_grad = weight_grad + paired(weight_grad, "z", 2)

    def near_terms(offset, sign, received):
        return call(
            functools.partial(spread_near_kernel, offset, sign),
            tables + (grads, received),
            table_specs + [VMEM] * 2,
            arrays(1, whole),
            scratch=[total],
            flops=18 * tile_flops,
        )[0]

    even_in, _ = lax.optimization_barrier((even_in, weight_grad))
    odd_near = near_terms(1, 2, even_in)
    odd_last = odd_swap(odd_near)
    odd_in, _ = lax.optimization_barrier((odd_in, odd_near))
    even_near = near_terms(3, -2, odd_in)
    even_last = even_swap(even_near)
    moved = paired(weight_grad, "yh", 1)
    moved, _, *output = lax.optimization_barrier((moved, even_near, *output))
    output = swapped(output)
    weight_grad = weight_grad + moved
    moved = [paired(weight_grad, "z", step) for step in (4, 12, 8)]
    weight_grad = weight_grad + moved[0] + moved[1] + moved[2]
    feature_grad, output = call(
        spread_own_kernel,
        tables + (grads, even_last, odd_last, *output),
        table_specs + [VMEM] * (3 + n_cols),
        arrays(2, whole),
        scratch=[total],
        flops=18 * tile_flops,
    )
    weight_grad, feature_grad = lax.optimization_barrier((weight_grad, feature_grad))
    weight_grad = summed(weight_grad, "x")
    weight_grad = (weight_grad * (1.0 / (node_count * n_rows) ** 0.5)).T
    return (output.T, feature_grad.T, weight_grad)


def solution(mesh):
    n_rows, n_cols = mesh.shape["rows"], mesh.shape["cols"]
    devices = mesh.devices.reshape(2, n_rows // 8, 4, 2, n_cols // 2)
    fine = Mesh(devices, ROWS + COLS)
    in_specs = (
        P(ROWS, COLS),
        P(None, COLS),
        P(ROWS, None, None),
        P(ROWS),
        P(ROWS),
        P(ROWS),
        P(ROWS, COLS),
    )
    out_specs = (P(ROWS, COLS), P(ROWS, COLS), P(None, COLS))
    return jax.shard_map(local, mesh=fine, in_specs=in_specs, out_specs=out_specs, check_vma=False)
```

```python
import functools

import jax
import jax.numpy as jnp
from jax import lax
from jax.experimental import pallas as pl
from jax.experimental.pallas import tpu as pltpu
from jax.sharding import Mesh, PartitionSpec as P

ROWS = ("yh", "z", "x")
COLS = ("yl", "core")
BLOCK = 128
NEAR = 5
VMEM = pl.BlockSpec(memory_space=pltpu.VMEM)
SMEM = pl.BlockSpec(memory_space=pltpu.SMEM)
BATCH = 6
PARTNERS = (0, 3, 2, 1)


def swap_pairs(count, odd):
    pairs = []
    for first in range(odd, count, 2):
        second = (first + 1) % count
        pairs += [(first, second), (second, first)]
    return pairs


def lanes(index):
    return pl.ds(pl.multiple_of(index * BLOCK, BLOCK), BLOCK)


def wide_lanes(index, width):
    return pl.ds(pl.multiple_of(index * width, width), width)


def each_tile(offset, count, values_ref, term, add):
    slots = values_ref.shape[0]
    per_offset = -(-slots // NEAR)
    for first in range(0, per_offset, BATCH):
        held = []
        for k in range(first, min(first + BATCH, per_offset)):
            slot = k * NEAR + offset
            live = (slot < count).astype(jnp.float32)
            slot = jnp.minimum(slot, slots - 1)
            held.append((slot, term(slot) * live))
        for slot, product in held:
            add(slot, product)


def gather_terms(info, source_ref, total_ref, offset):
    values_ref, rows_ref, cols_ref, count = info
    blocks = source_ref.shape[1] // BLOCK

    def term(slot):
        source = source_ref[:, lanes(lax.rem(cols_ref[slot], blocks))]
        return lax.dot_general(
            source, values_ref[slot], (((1,), (1,)), ((), ())), preferred_element_type=jnp.float32
        )

    def add(slot, product):
        where = lanes(rows_ref[slot])
        total_ref[:, where] = total_ref[:, where] + product

    each_tile(offset, count, values_ref, term, add)


def first_kernel(values, rows, cols, count, place, own, even, total):
    total[...] = jnp.zeros_like(total)
    info = (values, rows, cols, count[0])
    gather_terms(info, own, total, 2)
    gather_terms(info, even, total, 3 - 2 * place[0])


def second_kernel(values, rows, cols, count, place, start, odd, total):
    total[...] = start[...]
    gather_terms((values, rows, cols, count[0]), odd, total, 1 + 2 * place[0])


def pack_kernel(place, cotangent, weight, *packed):
    width = packed[0].shape[1] - weight.shape[1]
    for step, out in enumerate(packed):
        out[:, :width] = cotangent[:, wide_lanes(place[1] ^ PARTNERS[step], width)]
        out[:, width:] = weight[...]


def far_kernel(values, rows, cols, count, place, start, even, odd, *rest):
    hidden, total = rest[:-1], rest[-1]
    total[...] = start[...]
    info = (values, rows, cols, count[0])
    even_offset = 4 - 4 * place[0]
    gather_terms(info, even, total, even_offset)
    gather_terms(info, odd, total, 4 - even_offset)
    for step, out in enumerate(hidden):
        width = out.shape[1]
        out[...] = total[:, wide_lanes(place[1] ^ PARTNERS[step], width)].astype(out.dtype)


def dense_kernel(place, *refs):
    n = (len(refs) - 2) // 4
    hidden, given, sent, output = (refs[k * n : (k + 1) * n] for k in range(4))
    source_ref, back_ref = refs[4 * n :]
    cols, width = hidden[0].shape

    def group(step):
        return pl.ds(pl.multiple_of((place[1] ^ PARTNERS[step]) * cols, cols), cols)

    for step in range(n):
        source_ref[group(step), :] = hidden[step][...]
    source = source_ref[...]
    weight_t = jnp.concatenate([ref[:, width:] for ref in given], 0)
    preact = jnp.dot(weight_t, source, preferred_element_type=jnp.float32)
    sigmoid = 1.0 / (1.0 + jnp.exp(-preact))
    value = (preact * sigmoid).astype(jnp.bfloat16)
    slope = sigmoid * (1.0 + preact * (1.0 - sigmoid))
    grad = jnp.concatenate([ref[:, :width] for ref in given], 0).astype(jnp.float32) * slope
    grad = grad.astype(jnp.bfloat16)
    back = lax.dot_general(
        weight_t, grad, (((0,), (0,)), ((), ())), preferred_element_type=jnp.float32
    )
    back_ref[...] = back.astype(back_ref.dtype)
    weight_term = lax.dot_general(
        grad, source, (((1,), (1,)), ((), ())), preferred_element_type=jnp.float32
    ).astype(jnp.bfloat16)
    for step in range(n):
        here = slice(step * cols, (step + 1) * cols)
        output[step][...] = value[here]
        sent[step][:, :width] = back_ref[group(step), :]
        sent[step][:, width:] = weight_term[here]


def spread_terms(info, grad_ref, total_ref, offset):
    values_ref, rows_ref, cols_ref, count = info
    blocks = total_ref.shape[1] // BLOCK
    per_part = blocks // grad_ref.shape[0]

    def term(slot):
        row = rows_ref[slot]
        part = row // per_part
        source = grad_ref[part, :, lanes(row - part * per_part)]
        return jnp.dot(source, values_ref[slot], preferred_element_type=jnp.float32)

    def add(slot, product):
        where = lanes(lax.rem(cols_ref[slot], blocks))
        total_ref[:, where] = total_ref[:, where] + product

    each_tile(offset, count, values_ref, term, add)


def spread_far_kernel(values, rows, cols, count, place, *refs):
    n = len(refs) - 5
    sent = refs[:n]
    even, odd, grads, even_total, odd_total = refs[n:]
    width = grads.shape[2]
    for step, ref in enumerate(sent):
        grads[place[1] ^ PARTNERS[step]] = ref[:, :width]
    info = (values, rows, cols, count[0])
    even_offset = 4 - 4 * place[0]
    for offset, total, out in ((even_offset, even_total, even), (4 - even_offset, odd_total, odd)):
        total[...] = jnp.zeros_like(total)
        spread_terms(info, grads, total, offset)
        out[...] = total[...].astype(out.dtype)


def spread_near_kernel(offset, sign, values, rows, cols, count, place, grad, received, out, total):
    total[...] = received[...].astype(total.dtype)
    spread_terms((values, rows, cols, count[0]), grad, total, offset + sign * place[0])
    out[...] = total[...].astype(out.dtype)


def spread_own_kernel(values, rows, cols, count, place, grad, from_even, from_odd, *refs):
    parts, (out, output, total) = refs[:-3], refs[-3:]
    info = (values, rows, cols, count[0])
    total[...] = from_even[...].astype(total.dtype) + from_odd[...].astype(total.dtype)
    spread_terms(info, grad, total, 2)
    out[...] = total[...].astype(out.dtype)
    for step, part in enumerate(parts):
        output[:, wide_lanes(place[1] ^ PARTNERS[step], part.shape[1])] = part[...]


def call(kernel, args, specs, outs, scratch=(), flops=0):
    moved = sum(a.size * a.dtype.itemsize for a in args)
    moved += sum(o.size * o.dtype.itemsize for o in outs)
    return pl.pallas_call(
        kernel,
        out_shape=outs,
        in_specs=specs,
        out_specs=[VMEM] * len(outs),
        scratch_shapes=scratch,
        cost_estimate=pl.CostEstimate(flops=flops, bytes_accessed=moved, transcendentals=0),
        compiler_params=pltpu.CompilerParams(vmem_limit_bytes=24 << 20),
    )(*args)


def swapped(values):
    def pairs(step):
        return [(source, source ^ PARTNERS[step]) for source in range(len(values))]

    return [values[0]] + [
        lax.ppermute(value, COLS, pairs(step)) for step, value in enumerate(values) if step
    ]


def summed(value, axis):
    copies = jnp.broadcast_to(value, (lax.axis_size(axis), *value.shape))
    return lax.all_to_all(copies, axis, 0, 0, tiled=True).sum(0)


def paired(value, axis, step):
    count = lax.axis_size(axis)
    return lax.ppermute(value, axis, [(source, source ^ step) for source in range(count)])


def local(features, weight, tile_values, tile_rows, tile_cols, tile_count, cotangent):
    node_count, feat_cols = features.shape
    slots, tile, _ = tile_values.shape
    n_rows = lax.axis_size(ROWS)
    n_cols = lax.axis_size(COLS)
    width = node_count // n_cols
    full = feat_cols * n_cols
    even_pairs = swap_pairs(n_rows, 0)
    odd_pairs = swap_pairs(n_rows, 1)

    def even_swap(value):
        return lax.ppermute(value, ROWS, even_pairs)

    def odd_swap(value):
        return lax.ppermute(value, ROWS, odd_pairs)

    place = jnp.stack([lax.rem(lax.axis_index("x"), 2), lax.axis_index(COLS)]).astype(jnp.int32)
    tables = (tile_values, tile_rows, tile_cols, tile_count, place)
    table_specs = [VMEM, SMEM, SMEM, SMEM, SMEM]
    tile_flops = 2 * tile * tile * feat_cols

    def arrays(number, shape, dtype=jnp.bfloat16):
        return [jax.ShapeDtypeStruct(shape, dtype)] * number

    whole = (feat_cols, node_count)
    total = pltpu.VMEM(whole, jnp.float32)

    own = features.T
    even1 = even_swap(own)
    odd1 = odd_swap(own)
    given = call(
        pack_kernel,
        (place, cotangent.T, weight.T),
        [SMEM, VMEM, VMEM],
        arrays(n_cols, (feat_cols, width + full)),
    )
    even1, _ = lax.optimization_barrier((even1, given[0]))
    given = swapped(given)
    odd2 = odd_swap(even1)
    (first,) = call(
        first_kernel,
        tables + (own, even1),
        table_specs + [VMEM] * 2,
        arrays(1, whole, jnp.float32),
        flops=36 * tile_flops,
    )
    odd1, first = lax.optimization_barrier((odd1, first))
    even2 = even_swap(odd1)
    (near,) = call(
        second_kernel,
        tables + (first, odd1),
        table_specs + [VMEM] * 2,
        arrays(1, whole, jnp.float32),
        flops=18 * tile_flops,
    )
    hidden = call(
        far_kernel,
        tables + (near, even2, odd2),
        table_specs + [VMEM] * 3,
        arrays(n_cols, (feat_cols, width)),
        scratch=[total],
        flops=36 * tile_flops,
    )
    both = call(
        dense_kernel,
        (place, *swapped(hidden), *given),
        [SMEM] + [VMEM] * (2 * n_cols),
        arrays(n_cols, (feat_cols, width + full)) + arrays(n_cols, (feat_cols, width)),
        scratch=[pltpu.VMEM((full, width), jnp.bfloat16)] * 2,
        flops=6 * full * full * width,
    )
    output, sent = both[n_cols:], swapped(both[:n_cols])
    terms = [value[:, width:].astype(jnp.float32) for value in sent]
    weight_grad = sum(terms[1:], terms[0])
    even_far, odd_far, grads = call(
        spread_far_kernel,
        tables + tuple(sent),
        table_specs + [VMEM] * n_cols,
        arrays(2, whole) + arrays(1, (n_cols, feat_cols, width)),
        scratch=[total, total],
        flops=36 * tile_flops,
    )
    even_in = even_swap(even_far)
    odd_in = odd_swap(odd_far)
    weight_grad, _ = lax.optimization_barrier((weight_grad, even_far))
    weight_grad = weight_grad + paired(weight_grad, "yh", 1)
    weight_grad = weight_grad + paired(weight_grad, "z", 1)

    def near_terms(offset, sign, received):
        return call(
            functools.partial(spread_near_kernel, offset, sign),
            tables + (grads, received),
            table_specs + [VMEM] * 2,
            arrays(1, whole),
            scratch=[total],
            flops=18 * tile_flops,
        )[0]

    even_in, _ = lax.optimization_barrier((even_in, weight_grad))
    odd_near = near_terms(1, 2, even_in)
    odd_last = odd_swap(odd_near)
    weight_grad = weight_grad + paired(weight_grad, "z", 2)
    output = swapped(output)
    odd_in, *_ = lax.optimization_barrier((odd_in, odd_near, weight_grad, *output))
    even_near = near_terms(3, -2, odd_in)
    even_last = even_swap(even_near)
    weight_grad, _ = lax.optimization_barrier((weight_grad, even_near))
    moved = [paired(weight_grad, "z", step) for step in (4, 12, 8)]
    weight_grad = weight_grad + moved[0] + moved[1] + moved[2]
    feature_grad, output = call(
        spread_own_kernel,
        tables + (grads, even_last, odd_last, *output),
        table_specs + [VMEM] * (3 + n_cols),
        arrays(2, whole),
        scratch=[total],
        flops=18 * tile_flops,
    )
    weight_grad, feature_grad = lax.optimization_barrier((weight_grad, feature_grad))
    weight_grad = summed(weight_grad, "x")
    weight_grad = (weight_grad * (1.0 / (node_count * n_rows) ** 0.5)).T
    return (output.T, feature_grad.T, weight_grad)


def solution(mesh):
    n_rows, n_cols = mesh.shape["rows"], mesh.shape["cols"]
    devices = mesh.devices.reshape(2, n_rows // 8, 4, 2, n_cols // 2)
    fine = Mesh(devices, ROWS + COLS)
    in_specs = (
        P(ROWS, COLS),
        P(None, COLS),
        P(ROWS, None, None),
        P(ROWS),
        P(ROWS),
        P(ROWS),
        P(ROWS, COLS),
    )
    out_specs = (P(ROWS, COLS), P(ROWS, COLS), P(None, COLS))
    return jax.shard_map(local, mesh=fine, in_specs=in_specs, out_specs=out_specs, check_vma=False)
```

```python
import functools

import jax
import jax.numpy as jnp
from jax import lax
from jax.experimental import pallas as pl
from jax.experimental.pallas import tpu as pltpu
from jax.sharding import Mesh, PartitionSpec as P

ROWS = ("yh", "z", "x")
COLS = ("yl", "core")
BLOCK = 128
NEAR = 5
VMEM = pl.BlockSpec(memory_space=pltpu.VMEM)
SMEM = pl.BlockSpec(memory_space=pltpu.SMEM)
BATCH = 6
PARTNERS = (0, 3, 2, 1)


def swap_pairs(count, odd):
    pairs = []
    for first in range(odd, count, 2):
        second = (first + 1) % count
        pairs += [(first, second), (second, first)]
    return pairs


def lanes(index):
    return pl.ds(pl.multiple_of(index * BLOCK, BLOCK), BLOCK)


def wide_lanes(index, width):
    return pl.ds(pl.multiple_of(index * width, width), width)


def each_tile(offset, count, values_ref, term, add):
    slots = values_ref.shape[0]
    per_offset = -(-slots // NEAR)
    for first in range(0, per_offset, BATCH):
        held = []
        for k in range(first, min(first + BATCH, per_offset)):
            slot = k * NEAR + offset
            live = (slot < count).astype(jnp.float32)
            slot = jnp.minimum(slot, slots - 1)
            held.append((slot, term(slot) * live))
        for slot, product in held:
            add(slot, product)


def gather_terms(info, source_ref, total_ref, offset):
    values_ref, rows_ref, cols_ref, count = info
    blocks = source_ref.shape[1] // BLOCK

    def term(slot):
        source = source_ref[:, lanes(lax.rem(cols_ref[slot], blocks))]
        return lax.dot_general(
            source, values_ref[slot], (((1,), (1,)), ((), ())), preferred_element_type=jnp.float32
        )

    def add(slot, product):
        where = lanes(rows_ref[slot])
        total_ref[:, where] = total_ref[:, where] + product

    each_tile(offset, count, values_ref, term, add)


def first_kernel(values, rows, cols, count, place, own, even, total):
    total[...] = jnp.zeros_like(total)
    info = (values, rows, cols, count[0])
    gather_terms(info, own, total, 2)
    gather_terms(info, even, total, 3 - 2 * place[0])


def second_kernel(values, rows, cols, count, place, start, odd, total):
    total[...] = start[...]
    gather_terms((values, rows, cols, count[0]), odd, total, 1 + 2 * place[0])


def pack_kernel(place, cotangent, weight, *packed):
    width = packed[0].shape[1] - weight.shape[1]
    for step, out in enumerate(packed):
        out[:, :width] = cotangent[:, wide_lanes(place[1] ^ PARTNERS[step], width)]
        out[:, width:] = weight[...]


def far_kernel(values, rows, cols, count, place, start, even, odd, *rest):
    hidden, total = rest[:-1], rest[-1]
    total[...] = start[...]
    info = (values, rows, cols, count[0])
    even_offset = 4 - 4 * place[0]
    gather_terms(info, even, total, even_offset)
    gather_terms(info, odd, total, 4 - even_offset)
    for step, out in enumerate(hidden):
        width = out.shape[1]
        out[...] = total[:, wide_lanes(place[1] ^ PARTNERS[step], width)].astype(out.dtype)


def dense_kernel(place, *refs):
    n = (len(refs) - 2) // 4
    hidden, given, sent, output = (refs[k * n : (k + 1) * n] for k in range(4))
    source_ref, back_ref = refs[4 * n :]
    cols, width = hidden[0].shape

    def group(step):
        return pl.ds(pl.multiple_of((place[1] ^ PARTNERS[step]) * cols, cols), cols)

    for step in range(n):
        source_ref[group(step), :] = hidden[step][...]
    source = source_ref[...]
    weight_t = jnp.concatenate([ref[:, width:] for ref in given], 0)
    preact = jnp.dot(weight_t, source, preferred_element_type=jnp.float32)
    sigmoid = 1.0 / (1.0 + jnp.exp(-preact))
    value = (preact * sigmoid).astype(jnp.bfloat16)
    slope = sigmoid * (1.0 + preact * (1.0 - sigmoid))
    grad = jnp.concatenate([ref[:, :width] for ref in given], 0).astype(jnp.float32) * slope
    grad = grad.astype(jnp.bfloat16)
    back = lax.dot_general(
        weight_t, grad, (((0,), (0,)), ((), ())), preferred_element_type=jnp.float32
    )
    back_ref[...] = back.astype(back_ref.dtype)
    weight_term = lax.dot_general(
        grad, source, (((1,), (1,)), ((), ())), preferred_element_type=jnp.float32
    ).astype(jnp.bfloat16)
    for step in range(n):
        here = slice(step * cols, (step + 1) * cols)
        output[step][...] = value[here]
        sent[step][:, :width] = back_ref[group(step), :]
        sent[step][:, width:] = weight_term[here]


def spread_terms(info, grad_ref, total_ref, offset):
    values_ref, rows_ref, cols_ref, count = info
    blocks = total_ref.shape[1] // BLOCK
    per_part = blocks // grad_ref.shape[0]

    def term(slot):
        row = rows_ref[slot]
        part = row // per_part
        source = grad_ref[part, :, lanes(row - part * per_part)]
        return jnp.dot(source, values_ref[slot], preferred_element_type=jnp.float32)

    def add(slot, product):
        where = lanes(lax.rem(cols_ref[slot], blocks))
        total_ref[:, where] = total_ref[:, where] + product

    each_tile(offset, count, values_ref, term, add)


def spread_far_kernel(values, rows, cols, count, place, *refs):
    n = len(refs) - 5
    sent = refs[:n]
    even, odd, grads, even_total, odd_total = refs[n:]
    width = grads.shape[2]
    for step, ref in enumerate(sent):
        grads[place[1] ^ PARTNERS[step]] = ref[:, :width]
    info = (values, rows, cols, count[0])
    even_offset = 4 - 4 * place[0]
    for offset, total, out in ((even_offset, even_total, even), (4 - even_offset, odd_total, odd)):
        total[...] = jnp.zeros_like(total)
        spread_terms(info, grads, total, offset)
        out[...] = total[...].astype(out.dtype)


def spread_near_kernel(offset, sign, values, rows, cols, count, place, grad, received, out, total):
    total[...] = received[...].astype(total.dtype)
    spread_terms((values, rows, cols, count[0]), grad, total, offset + sign * place[0])
    out[...] = total[...].astype(out.dtype)


def spread_own_kernel(values, rows, cols, count, place, grad, from_even, from_odd, *refs):
    parts, (out, output, total) = refs[:-3], refs[-3:]
    info = (values, rows, cols, count[0])
    total[...] = from_even[...].astype(total.dtype) + from_odd[...].astype(total.dtype)
    spread_terms(info, grad, total, 2)
    out[...] = total[...].astype(out.dtype)
    for step, part in enumerate(parts):
        output[:, wide_lanes(place[1] ^ PARTNERS[step], part.shape[1])] = part[...]


def call(kernel, args, specs, outs, scratch=(), flops=0):
    moved = sum(a.size * a.dtype.itemsize for a in args)
    moved += sum(o.size * o.dtype.itemsize for o in outs)
    return pl.pallas_call(
        kernel,
        out_shape=outs,
        in_specs=specs,
        out_specs=[VMEM] * len(outs),
        scratch_shapes=scratch,
        cost_estimate=pl.CostEstimate(flops=flops, bytes_accessed=moved, transcendentals=0),
        compiler_params=pltpu.CompilerParams(vmem_limit_bytes=24 << 20),
    )(*args)


def swapped(values):
    def pairs(step):
        return [(source, source ^ PARTNERS[step]) for source in range(len(values))]

    return [values[0]] + [
        lax.ppermute(value, COLS, pairs(step)) for step, value in enumerate(values) if step
    ]


def summed(value, axis):
    copies = jnp.broadcast_to(value, (lax.axis_size(axis), *value.shape))
    return lax.all_to_all(copies, axis, 0, 0, tiled=True).sum(0)


def paired(value, axis, step):
    count = lax.axis_size(axis)
    return lax.ppermute(value, axis, [(source, source ^ step) for source in range(count)])


def local(features, weight, tile_values, tile_rows, tile_cols, tile_count, cotangent):
    node_count, feat_cols = features.shape
    slots, tile, _ = tile_values.shape
    n_rows = lax.axis_size(ROWS)
    n_cols = lax.axis_size(COLS)
    width = node_count // n_cols
    full = feat_cols * n_cols
    even_pairs = swap_pairs(n_rows, 0)
    odd_pairs = swap_pairs(n_rows, 1)

    def even_swap(value):
        return lax.ppermute(value, ROWS, even_pairs)

    def odd_swap(value):
        return lax.ppermute(value, ROWS, odd_pairs)

    place = jnp.stack([lax.rem(lax.axis_index("x"), 2), lax.axis_index(COLS)]).astype(jnp.int32)
    tables = (tile_values, tile_rows, tile_cols, tile_count, place)
    table_specs = [VMEM, SMEM, SMEM, SMEM, SMEM]
    tile_flops = 2 * tile * tile * feat_cols

    def arrays(number, shape, dtype=jnp.bfloat16):
        return [jax.ShapeDtypeStruct(shape, dtype)] * number

    whole = (feat_cols, node_count)
    total = pltpu.VMEM(whole, jnp.float32)

    own = features.T
    even1 = even_swap(own)
    odd1 = odd_swap(own)
    given = call(
        pack_kernel,
        (place, cotangent.T, weight.T),
        [SMEM, VMEM, VMEM],
        arrays(n_cols, (feat_cols, width + full)),
    )
    even1, _ = lax.optimization_barrier((even1, given[0]))
    given = swapped(given)
    odd2 = odd_swap(even1)
    (first,) = call(
        first_kernel,
        tables + (own, even1),
        table_specs + [VMEM] * 2,
        arrays(1, whole, jnp.float32),
        flops=36 * tile_flops,
    )
    odd1, first = lax.optimization_barrier((odd1, first))
    even2 = even_swap(odd1)
    (near,) = call(
        second_kernel,
        tables + (first, odd1),
        table_specs + [VMEM] * 2,
        arrays(1, whole, jnp.float32),
        flops=18 * tile_flops,
    )
    hidden = call(
        far_kernel,
        tables + (near, even2, odd2),
        table_specs + [VMEM] * 3,
        arrays(n_cols, (feat_cols, width)),
        scratch=[total],
        flops=36 * tile_flops,
    )
    both = call(
        dense_kernel,
        (place, *swapped(hidden), *given),
        [SMEM] + [VMEM] * (2 * n_cols),
        arrays(n_cols, (feat_cols, width + full)) + arrays(n_cols, (feat_cols, width)),
        scratch=[pltpu.VMEM((full, width), jnp.bfloat16)] * 2,
        flops=6 * full * full * width,
    )
    output, sent = both[n_cols:], swapped(both[:n_cols])
    terms = [value[:, width:].astype(jnp.float32) for value in sent]
    weight_grad = sum(terms[1:], terms[0])
    even_far, odd_far, grads = call(
        spread_far_kernel,
        tables + tuple(sent),
        table_specs + [VMEM] * n_cols,
        arrays(2, whole) + arrays(1, (n_cols, feat_cols, width)),
        scratch=[total, total],
        flops=36 * tile_flops,
    )
    even_in = even_swap(even_far)
    odd_in = odd_swap(odd_far)
    weight_grad, _ = lax.optimization_barrier((weight_grad, even_far))
    weight_grad = weight_grad + paired(weight_grad, "z", 1)
    weight_grad = weight_grad + paired(weight_grad, "z", 2)

    def near_terms(offset, sign, received):
        return call(
            functools.partial(spread_near_kernel, offset, sign),
            tables + (grads, received),
            table_specs + [VMEM] * 2,
            arrays(1, whole),
            scratch=[total],
            flops=18 * tile_flops,
        )[0]

    even_in, _ = lax.optimization_barrier((even_in, weight_grad))
    odd_near = near_terms(1, 2, even_in)
    odd_last = odd_swap(odd_near)
    output = swapped(output)
    odd_in, *_ = lax.optimization_barrier((odd_in, odd_near, *output))
    even_near = near_terms(3, -2, odd_in)
    even_last = even_swap(even_near)
    moved = paired(weight_grad, "yh", 1)
    moved, _ = lax.optimization_barrier((moved, even_near))
    weight_grad = weight_grad + moved
    moved = [paired(weight_grad, "z", step) for step in (4, 12, 8)]
    weight_grad = weight_grad + moved[0] + moved[1] + moved[2]
    feature_grad, output = call(
        spread_own_kernel,
        tables + (grads, even_last, odd_last, *output),
        table_specs + [VMEM] * (3 + n_cols),
        arrays(2, whole),
        scratch=[total],
        flops=18 * tile_flops,
    )
    weight_grad, feature_grad = lax.optimization_barrier((weight_grad, feature_grad))
    weight_grad = summed(weight_grad, "x")
    weight_grad = (weight_grad * (1.0 / (node_count * n_rows) ** 0.5)).T
    return (output.T, feature_grad.T, weight_grad)


def solution(mesh):
    n_rows, n_cols = mesh.shape["rows"], mesh.shape["cols"]
    devices = mesh.devices.reshape(2, n_rows // 8, 4, 2, n_cols // 2)
    fine = Mesh(devices, ROWS + COLS)
    in_specs = (
        P(ROWS, COLS),
        P(None, COLS),
        P(ROWS, None, None),
        P(ROWS),
        P(ROWS),
        P(ROWS),
        P(ROWS, COLS),
    )
    out_specs = (P(ROWS, COLS), P(ROWS, COLS), P(None, COLS))
    return jax.shard_map(local, mesh=fine, in_specs=in_specs, out_specs=out_specs, check_vma=False)
```

```python
import functools

import jax
import jax.numpy as jnp
from jax import lax
from jax.experimental import pallas as pl
from jax.experimental.pallas import tpu as pltpu
from jax.sharding import Mesh, PartitionSpec as P

ROWS = ("yh", "z", "x")
COLS = ("yl", "core")
BLOCK = 128
NEAR = 5
VMEM = pl.BlockSpec(memory_space=pltpu.VMEM)
SMEM = pl.BlockSpec(memory_space=pltpu.SMEM)
BATCH = 6
PARTNERS = (0, 3, 2, 1)


def swap_pairs(count, odd):
    pairs = []
    for first in range(odd, count, 2):
        second = (first + 1) % count
        pairs += [(first, second), (second, first)]
    return pairs


def lanes(index):
    return pl.ds(pl.multiple_of(index * BLOCK, BLOCK), BLOCK)


def wide_lanes(index, width):
    return pl.ds(pl.multiple_of(index * width, width), width)


def each_tile(offset, count, values_ref, term, add):
    slots = values_ref.shape[0]
    per_offset = -(-slots // NEAR)
    for first in range(0, per_offset, BATCH):
        held = []
        for k in range(first, min(first + BATCH, per_offset)):
            slot = k * NEAR + offset
            live = (slot < count).astype(jnp.float32)
            slot = jnp.minimum(slot, slots - 1)
            held.append((slot, term(slot) * live))
        for slot, product in held:
            add(slot, product)


def gather_terms(info, source_ref, total_ref, offset):
    values_ref, rows_ref, cols_ref, count = info
    blocks = source_ref.shape[1] // BLOCK

    def term(slot):
        source = source_ref[:, lanes(lax.rem(cols_ref[slot], blocks))]
        return lax.dot_general(
            source, values_ref[slot], (((1,), (1,)), ((), ())), preferred_element_type=jnp.float32
        )

    def add(slot, product):
        where = lanes(rows_ref[slot])
        total_ref[:, where] = total_ref[:, where] + product

    each_tile(offset, count, values_ref, term, add)


def first_kernel(values, rows, cols, count, place, own, even, total):
    total[...] = jnp.zeros_like(total)
    info = (values, rows, cols, count[0])
    gather_terms(info, own, total, 2)
    gather_terms(info, even, total, 3 - 2 * place[0])


def second_kernel(values, rows, cols, count, place, start, odd, total):
    total[...] = start[...]
    gather_terms((values, rows, cols, count[0]), odd, total, 1 + 2 * place[0])


def pack_kernel(place, cotangent, weight, *packed):
    width = packed[0].shape[1] - weight.shape[1]
    for step, out in enumerate(packed):
        out[:, :width] = cotangent[:, wide_lanes(place[1] ^ PARTNERS[step], width)]
        out[:, width:] = weight[...]


def far_kernel(values, rows, cols, count, place, start, even, odd, *rest):
    hidden, total = rest[:-1], rest[-1]
    total[...] = start[...]
    info = (values, rows, cols, count[0])
    even_offset = 4 - 4 * place[0]
    gather_terms(info, even, total, even_offset)
    gather_terms(info, odd, total, 4 - even_offset)
    for step, out in enumerate(hidden):
        width = out.shape[1]
        out[...] = total[:, wide_lanes(place[1] ^ PARTNERS[step], width)].astype(out.dtype)


def dense_kernel(place, *refs):
    n = (len(refs) - 2) // 4
    hidden, given, sent, output = (refs[k * n : (k + 1) * n] for k in range(4))
    source_ref, back_ref = refs[4 * n :]
    cols, width = hidden[0].shape

    def group(step):
        return pl.ds(pl.multiple_of((place[1] ^ PARTNERS[step]) * cols, cols), cols)

    for step in range(n):
        source_ref[group(step), :] = hidden[step][...]
    source = source_ref[...]
    weight_t = jnp.concatenate([ref[:, width:] for ref in given], 0)
    preact = jnp.dot(weight_t, source, preferred_element_type=jnp.float32)
    sigmoid = 1.0 / (1.0 + jnp.exp(-preact))
    value = (preact * sigmoid).astype(jnp.bfloat16)
    slope = sigmoid * (1.0 + preact * (1.0 - sigmoid))
    grad = jnp.concatenate([ref[:, :width] for ref in given], 0).astype(jnp.float32) * slope
    grad = grad.astype(jnp.bfloat16)
    back = lax.dot_general(
        weight_t, grad, (((0,), (0,)), ((), ())), preferred_element_type=jnp.float32
    )
    back_ref[...] = back.astype(back_ref.dtype)
    weight_term = lax.dot_general(
        grad, source, (((1,), (1,)), ((), ())), preferred_element_type=jnp.float32
    ).astype(jnp.bfloat16)
    for step in range(n):
        here = slice(step * cols, (step + 1) * cols)
        output[step][...] = value[here]
        sent[step][:, :width] = back_ref[group(step), :]
        sent[step][:, width:] = weight_term[here]


def spread_terms(info, grad_ref, total_ref, offset):
    values_ref, rows_ref, cols_ref, count = info
    blocks = total_ref.shape[1] // BLOCK
    per_part = blocks // grad_ref.shape[0]

    def term(slot):
        row = rows_ref[slot]
        part = row // per_part
        source = grad_ref[part, :, lanes(row - part * per_part)]
        return jnp.dot(source, values_ref[slot], preferred_element_type=jnp.float32)

    def add(slot, product):
        where = lanes(lax.rem(cols_ref[slot], blocks))
        total_ref[:, where] = total_ref[:, where] + product

    each_tile(offset, count, values_ref, term, add)


def spread_far_kernel(values, rows, cols, count, place, *refs):
    n = len(refs) - 5
    sent = refs[:n]
    even, odd, grads, even_total, odd_total = refs[n:]
    width = grads.shape[2]
    for step, ref in enumerate(sent):
        grads[place[1] ^ PARTNERS[step]] = ref[:, :width]
    info = (values, rows, cols, count[0])
    even_offset = 4 - 4 * place[0]
    for offset, total, out in ((even_offset, even_total, even), (4 - even_offset, odd_total, odd)):
        total[...] = jnp.zeros_like(total)
        spread_terms(info, grads, total, offset)
        out[...] = total[...].astype(out.dtype)


def spread_near_kernel(offset, sign, values, rows, cols, count, place, grad, received, out, total):
    total[...] = received[...].astype(total.dtype)
    spread_terms((values, rows, cols, count[0]), grad, total, offset + sign * place[0])
    out[...] = total[...].astype(out.dtype)


def spread_own_kernel(values, rows, cols, count, place, grad, from_even, from_odd, *refs):
    parts, (out, output, total) = refs[:-3], refs[-3:]
    info = (values, rows, cols, count[0])
    total[...] = from_even[...].astype(total.dtype) + from_odd[...].astype(total.dtype)
    spread_terms(info, grad, total, 2)
    out[...] = total[...].astype(out.dtype)
    for step, part in enumerate(parts):
        output[:, wide_lanes(place[1] ^ PARTNERS[step], part.shape[1])] = part[...]


def call(kernel, args, specs, outs, scratch=(), flops=0):
    moved = sum(a.size * a.dtype.itemsize for a in args)
    moved += sum(o.size * o.dtype.itemsize for o in outs)
    return pl.pallas_call(
        kernel,
        out_shape=outs,
        in_specs=specs,
        out_specs=[VMEM] * len(outs),
        scratch_shapes=scratch,
        cost_estimate=pl.CostEstimate(flops=flops, bytes_accessed=moved, transcendentals=0),
        compiler_params=pltpu.CompilerParams(vmem_limit_bytes=24 << 20),
    )(*args)


def swapped(values):
    def pairs(step):
        return [(source, source ^ PARTNERS[step]) for source in range(len(values))]

    return [values[0]] + [
        lax.ppermute(value, COLS, pairs(step)) for step, value in enumerate(values) if step
    ]


def summed(value, axis):
    copies = jnp.broadcast_to(value.astype(jnp.bfloat16), (lax.axis_size(axis), *value.shape))
    return lax.all_to_all(copies, axis, 0, 0, tiled=True).astype(jnp.float32).sum(0)


def paired(value, axis, step):
    count = lax.axis_size(axis)
    return lax.ppermute(value, axis, [(source, source ^ step) for source in range(count)])


def local(features, weight, tile_values, tile_rows, tile_cols, tile_count, cotangent):
    node_count, feat_cols = features.shape
    slots, tile, _ = tile_values.shape
    n_rows = lax.axis_size(ROWS)
    n_cols = lax.axis_size(COLS)
    width = node_count // n_cols
    full = feat_cols * n_cols
    even_pairs = swap_pairs(n_rows, 0)
    odd_pairs = swap_pairs(n_rows, 1)

    def even_swap(value):
        return lax.ppermute(value, ROWS, even_pairs)

    def odd_swap(value):
        return lax.ppermute(value, ROWS, odd_pairs)

    place = jnp.stack([lax.rem(lax.axis_index("x"), 2), lax.axis_index(COLS)]).astype(jnp.int32)
    tables = (tile_values, tile_rows, tile_cols, tile_count, place)
    table_specs = [VMEM, SMEM, SMEM, SMEM, SMEM]
    tile_flops = 2 * tile * tile * feat_cols

    def arrays(number, shape, dtype=jnp.bfloat16):
        return [jax.ShapeDtypeStruct(shape, dtype)] * number

    whole = (feat_cols, node_count)
    total = pltpu.VMEM(whole, jnp.float32)

    own = features.T
    even1 = even_swap(own)
    odd1 = odd_swap(own)
    given = call(
        pack_kernel,
        (place, cotangent.T, weight.T),
        [SMEM, VMEM, VMEM],
        arrays(n_cols, (feat_cols, width + full)),
    )
    even1, _ = lax.optimization_barrier((even1, given[0]))
    given = swapped(given)
    odd2 = odd_swap(even1)
    (first,) = call(
        first_kernel,
        tables + (own, even1),
        table_specs + [VMEM] * 2,
        arrays(1, whole, jnp.float32),
        flops=36 * tile_flops,
    )
    odd1, first = lax.optimization_barrier((odd1, first))
    even2 = even_swap(odd1)
    (near,) = call(
        second_kernel,
        tables + (first, odd1),
        table_specs + [VMEM] * 2,
        arrays(1, whole, jnp.float32),
        flops=18 * tile_flops,
    )
    hidden = call(
        far_kernel,
        tables + (near, even2, odd2),
        table_specs + [VMEM] * 3,
        arrays(n_cols, (feat_cols, width)),
        scratch=[total],
        flops=36 * tile_flops,
    )
    both = call(
        dense_kernel,
        (place, *swapped(hidden), *given),
        [SMEM] + [VMEM] * (2 * n_cols),
        arrays(n_cols, (feat_cols, width + full)) + arrays(n_cols, (feat_cols, width)),
        scratch=[pltpu.VMEM((full, width), jnp.bfloat16)] * 2,
        flops=6 * full * full * width,
    )
    output, sent = both[n_cols:], swapped(both[:n_cols])
    terms = [value[:, width:].astype(jnp.float32) for value in sent]
    weight_grad = sum(terms[1:], terms[0])
    even_far, odd_far, grads = call(
        spread_far_kernel,
        tables + tuple(sent),
        table_specs + [VMEM] * n_cols,
        arrays(2, whole) + arrays(1, (n_cols, feat_cols, width)),
        scratch=[total, total],
        flops=36 * tile_flops,
    )
    even_in = even_swap(even_far)
    odd_in = odd_swap(odd_far)
    weight_grad, _ = lax.optimization_barrier((weight_grad, even_far))
    weight_grad = weight_grad + paired(weight_grad, "z", 1)
    weight_grad = weight_grad + paired(weight_grad, "z", 2)

    def near_terms(offset, sign, received):
        return call(
            functools.partial(spread_near_kernel, offset, sign),
            tables + (grads, received),
            table_specs + [VMEM] * 2,
            arrays(1, whole),
            scratch=[total],
            flops=18 * tile_flops,
        )[0]

    even_in, _ = lax.optimization_barrier((even_in, weight_grad))
    odd_near = near_terms(1, 2, even_in)
    odd_last = odd_swap(odd_near)
    output = swapped(output)
    odd_in, *_ = lax.optimization_barrier((odd_in, odd_near, *output))
    even_near = near_terms(3, -2, odd_in)
    even_last = even_swap(even_near)
    weight_grad, _ = lax.optimization_barrier((weight_grad, even_near))
    moved = [paired(weight_grad, "z", step) for step in (4, 12, 8)]
    weight_grad = (weight_grad + moved[2]) + (moved[0] + moved[1])
    feature_grad, output = call(
        spread_own_kernel,
        tables + (grads, even_last, odd_last, *output),
        table_specs + [VMEM] * (3 + n_cols),
        arrays(2, whole),
        scratch=[total],
        flops=18 * tile_flops,
    )
    weight_grad, feature_grad = lax.optimization_barrier((weight_grad, feature_grad))
    weight_grad = summed(weight_grad, ("yh", "x"))
    weight_grad = (weight_grad * (1.0 / (node_count * n_rows) ** 0.5)).T
    return (output.T, feature_grad.T, weight_grad)


def solution(mesh):
    n_rows, n_cols = mesh.shape["rows"], mesh.shape["cols"]
    devices = mesh.devices.reshape(2, n_rows // 8, 4, 2, n_cols // 2)
    fine = Mesh(devices, ROWS + COLS)
    in_specs = (
        P(ROWS, COLS),
        P(None, COLS),
        P(ROWS, None, None),
        P(ROWS),
        P(ROWS),
        P(ROWS),
        P(ROWS, COLS),
    )
    out_specs = (P(ROWS, COLS), P(ROWS, COLS), P(None, COLS))
    return jax.shard_map(local, mesh=fine, in_specs=in_specs, out_specs=out_specs, check_vma=False)
```

```python
import functools

import jax
import jax.numpy as jnp
from jax import lax
from jax.experimental import pallas as pl
from jax.experimental.pallas import tpu as pltpu
from jax.sharding import Mesh, PartitionSpec as P

ROWS = ("yh", "z", "x")
COLS = ("yl", "core")
BLOCK = 128
NEAR = 5
VMEM = pl.BlockSpec(memory_space=pltpu.VMEM)
SMEM = pl.BlockSpec(memory_space=pltpu.SMEM)
BATCH = 6
PARTNERS = (0, 3, 2, 1)


def swap_pairs(count, odd):
    pairs = []
    for first in range(odd, count, 2):
        second = (first + 1) % count
        pairs += [(first, second), (second, first)]
    return pairs


def lanes(index):
    return pl.ds(pl.multiple_of(index * BLOCK, BLOCK), BLOCK)


def wide_lanes(index, width):
    return pl.ds(pl.multiple_of(index * width, width), width)


def each_tile(offset, count, values_ref, term, add):
    slots = values_ref.shape[0]
    per_offset = -(-slots // NEAR)
    for first in range(0, per_offset, BATCH):
        held = []
        for k in range(first, min(first + BATCH, per_offset)):
            slot = k * NEAR + offset
            live = (slot < count).astype(jnp.float32)
            slot = jnp.minimum(slot, slots - 1)
            held.append((slot, term(slot) * live))
        for slot, product in held:
            add(slot, product)


def gather_terms(info, source_refs, total_ref, offset):
    values_ref, rows_ref, cols_ref, count = info
    blocks = total_ref.shape[1] // BLOCK

    def term(slot):
        where = lanes(lax.rem(cols_ref[slot], blocks))
        source = jnp.concatenate([ref[:, where] for ref in source_refs], 0)
        return lax.dot_general(
            source, values_ref[slot], (((1,), (1,)), ((), ())), preferred_element_type=jnp.float32
        )

    def add(slot, product):
        where = lanes(rows_ref[slot])
        total_ref[:, where] = total_ref[:, where] + product

    each_tile(offset, count, values_ref, term, add)


def first_kernel(values, rows, cols, count, place, own_a, own_b, even_a, even_b, total):
    total[...] = jnp.zeros_like(total)
    info = (values, rows, cols, count[0])
    gather_terms(info, [own_a, own_b], total, 2)
    gather_terms(info, [even_a, even_b], total, 3 - 2 * place[0])


def second_kernel(values, rows, cols, count, place, start, odd_a, odd_b, total):
    total[...] = start[...]
    gather_terms((values, rows, cols, count[0]), [odd_a, odd_b], total, 1 + 2 * place[0])


def pack_kernel(place, cotangent, weight, *packed):
    width = packed[0].shape[1] - weight.shape[1]
    for step, out in enumerate(packed):
        out[:, :width] = cotangent[:, wide_lanes(place[1] ^ PARTNERS[step], width)]
        out[:, width:] = weight[...]


def far_kernel(values, rows, cols, count, place, start, even_a, even_b, odd_a, odd_b, *rest):
    hidden, total = rest[:-1], rest[-1]
    total[...] = start[...]
    info = (values, rows, cols, count[0])
    even_offset = 4 - 4 * place[0]
    gather_terms(info, [even_a, even_b], total, even_offset)
    gather_terms(info, [odd_a, odd_b], total, 4 - even_offset)
    for step, out in enumerate(hidden):
        width = out.shape[1]
        out[...] = total[:, wide_lanes(place[1] ^ PARTNERS[step], width)].astype(out.dtype)


def dense_kernel(place, *refs):
    n = (len(refs) - 2) // 4
    hidden, given, sent, output = (refs[k * n : (k + 1) * n] for k in range(4))
    source_ref, back_ref = refs[4 * n :]
    cols, width = hidden[0].shape

    def group(step):
        return pl.ds(pl.multiple_of((place[1] ^ PARTNERS[step]) * cols, cols), cols)

    for step in range(n):
        source_ref[group(step), :] = hidden[step][...]
    source = source_ref[...]
    weight_t = jnp.concatenate([ref[:, width:] for ref in given], 0)
    preact = jnp.dot(weight_t, source, preferred_element_type=jnp.float32)
    sigmoid = 1.0 / (1.0 + jnp.exp(-preact))
    value = (preact * sigmoid).astype(jnp.bfloat16)
    slope = sigmoid * (1.0 + preact * (1.0 - sigmoid))
    grad = jnp.concatenate([ref[:, :width] for ref in given], 0).astype(jnp.float32) * slope
    grad = grad.astype(jnp.bfloat16)
    back = lax.dot_general(
        weight_t, grad, (((0,), (0,)), ((), ())), preferred_element_type=jnp.float32
    )
    back_ref[...] = back.astype(back_ref.dtype)
    weight_term = lax.dot_general(
        grad, source, (((1,), (1,)), ((), ())), preferred_element_type=jnp.float32
    ).astype(jnp.bfloat16)
    for step in range(n):
        here = slice(step * cols, (step + 1) * cols)
        output[step][...] = value[here]
        sent[step][:, :width] = back_ref[group(step), :]
        sent[step][:, width:] = weight_term[here]


def spread_terms(info, grad_ref, total_ref, offset):
    values_ref, rows_ref, cols_ref, count = info
    blocks = total_ref.shape[1] // BLOCK
    per_part = blocks // grad_ref.shape[0]

    def term(slot):
        row = rows_ref[slot]
        part = row // per_part
        source = grad_ref[part, :, lanes(row - part * per_part)]
        return jnp.dot(source, values_ref[slot], preferred_element_type=jnp.float32)

    def add(slot, product):
        where = lanes(lax.rem(cols_ref[slot], blocks))
        total_ref[:, where] = total_ref[:, where] + product

    each_tile(offset, count, values_ref, term, add)


def spread_far_kernel(values, rows, cols, count, place, *refs):
    n = len(refs) - 5
    sent = refs[:n]
    even, odd, grads, even_total, odd_total = refs[n:]
    width = grads.shape[2]
    for step, ref in enumerate(sent):
        grads[place[1] ^ PARTNERS[step]] = ref[:, :width]
    info = (values, rows, cols, count[0])
    even_offset = 4 - 4 * place[0]
    for offset, total, out in ((even_offset, even_total, even), (4 - even_offset, odd_total, odd)):
        total[...] = jnp.zeros_like(total)
        spread_terms(info, grads, total, offset)
        out[...] = total[...].astype(out.dtype)


def spread_near_kernel(offset, sign, values, rows, cols, count, place, grad, received, out, total):
    total[...] = received[...].astype(total.dtype)
    spread_terms((values, rows, cols, count[0]), grad, total, offset + sign * place[0])
    out[...] = total[...].astype(out.dtype)


def spread_own_kernel(values, rows, cols, count, place, grad, from_even, from_odd, *refs):
    parts, (out, output, total) = refs[:-3], refs[-3:]
    info = (values, rows, cols, count[0])
    total[...] = from_even[...].astype(total.dtype) + from_odd[...].astype(total.dtype)
    spread_terms(info, grad, total, 2)
    out[...] = total[...].astype(out.dtype)
    for step, part in enumerate(parts):
        output[:, wide_lanes(place[1] ^ PARTNERS[step], part.shape[1])] = part[...]


def call(kernel, args, specs, outs, scratch=(), flops=0):
    moved = sum(a.size * a.dtype.itemsize for a in args)
    moved += sum(o.size * o.dtype.itemsize for o in outs)
    return pl.pallas_call(
        kernel,
        out_shape=outs,
        in_specs=specs,
        out_specs=[VMEM] * len(outs),
        scratch_shapes=scratch,
        cost_estimate=pl.CostEstimate(flops=flops, bytes_accessed=moved, transcendentals=0),
        compiler_params=pltpu.CompilerParams(vmem_limit_bytes=24 << 20),
    )(*args)


def swapped(values):
    def pairs(step):
        return [(source, source ^ PARTNERS[step]) for source in range(len(values))]

    return [values[0]] + [
        lax.ppermute(value, COLS, pairs(step)) for step, value in enumerate(values) if step
    ]


def summed(value, axis):
    copies = jnp.broadcast_to(value.astype(jnp.bfloat16), (lax.axis_size(axis), *value.shape))
    return lax.all_to_all(copies, axis, 0, 0, tiled=True).astype(jnp.float32).sum(0)


def paired(value, axis, step):
    count = lax.axis_size(axis)
    return lax.ppermute(value, axis, [(source, source ^ step) for source in range(count)])


def local(features, weight, tile_values, tile_rows, tile_cols, tile_count, cotangent):
    node_count, feat_cols = features.shape
    slots, tile, _ = tile_values.shape
    n_rows = lax.axis_size(ROWS)
    n_cols = lax.axis_size(COLS)
    width = node_count // n_cols
    full = feat_cols * n_cols
    even_pairs = swap_pairs(n_rows, 0)
    odd_pairs = swap_pairs(n_rows, 1)

    def even_swap(value):
        return lax.ppermute(value, ROWS, even_pairs)

    def odd_swap(value):
        return lax.ppermute(value, ROWS, odd_pairs)

    place = jnp.stack([lax.rem(lax.axis_index("x"), 2), lax.axis_index(COLS)]).astype(jnp.int32)
    tables = (tile_values, tile_rows, tile_cols, tile_count, place)
    table_specs = [VMEM, SMEM, SMEM, SMEM, SMEM]
    tile_flops = 2 * tile * tile * feat_cols

    def arrays(number, shape, dtype=jnp.bfloat16):
        return [jax.ShapeDtypeStruct(shape, dtype)] * number

    whole = (feat_cols, node_count)
    total = pltpu.VMEM(whole, jnp.float32)

    own = features.T
    half = feat_cols // 2
    even1, odd1 = [], []
    own = (own[:half], own[half:])
    for piece in own:
        even1.append(even_swap(piece))
        odd1.append(odd_swap(piece))
    given = call(
        pack_kernel,
        (place, cotangent.T, weight.T),
        [SMEM, VMEM, VMEM],
        arrays(n_cols, (feat_cols, width + full)),
    )
    even1[0], _ = lax.optimization_barrier((even1[0], given[0]))
    given = swapped(given)
    odd2 = [odd_swap(piece) for piece in even1]
    even2 = [even_swap(piece) for piece in odd1]
    (first,) = call(
        first_kernel,
        tables + (*own, *even1),
        table_specs + [VMEM] * 4,
        arrays(1, whole, jnp.float32),
        flops=36 * tile_flops,
    )
    (near,) = call(
        second_kernel,
        tables + (first, *odd1),
        table_specs + [VMEM] * 3,
        arrays(1, whole, jnp.float32),
        flops=18 * tile_flops,
    )
    hidden = call(
        far_kernel,
        tables + (near, *even2, *odd2),
        table_specs + [VMEM] * 5,
        arrays(n_cols, (feat_cols, width)),
        scratch=[total],
        flops=36 * tile_flops,
    )
    both = call(
        dense_kernel,
        (place, *swapped(hidden), *given),
        [SMEM] + [VMEM] * (2 * n_cols),
        arrays(n_cols, (feat_cols, width + full)) + arrays(n_cols, (feat_cols, width)),
        scratch=[pltpu.VMEM((full, width), jnp.bfloat16)] * 2,
        flops=6 * full * full * width,
    )
    output, sent = both[n_cols:], swapped(both[:n_cols])
    terms = [value[:, width:].astype(jnp.float32) for value in sent]
    weight_grad = sum(terms[1:], terms[0])
    even_far, odd_far, grads = call(
        spread_far_kernel,
        tables + tuple(sent),
        table_specs + [VMEM] * n_cols,
        arrays(2, whole) + arrays(1, (n_cols, feat_cols, width)),
        scratch=[total, total],
        flops=36 * tile_flops,
    )
    even_in = even_swap(even_far)
    odd_in = odd_swap(odd_far)
    weight_grad, _ = lax.optimization_barrier((weight_grad, even_far))
    weight_grad = weight_grad + paired(weight_grad, "z", 1)
    weight_grad = weight_grad + paired(weight_grad, "z", 2)

    def near_terms(offset, sign, received):
        return call(
            functools.partial(spread_near_kernel, offset, sign),
            tables + (grads, received),
            table_specs + [VMEM] * 2,
            arrays(1, whole),
            scratch=[total],
            flops=18 * tile_flops,
        )[0]

    even_in, _ = lax.optimization_barrier((even_in, weight_grad))
    odd_near = near_terms(1, 2, even_in)
    odd_last = odd_swap(odd_near)
    output = swapped(output)
    odd_in, *_ = lax.optimization_barrier((odd_in, odd_near, *output))
    even_near = near_terms(3, -2, odd_in)
    even_last = even_swap(even_near)
    weight_grad, _ = lax.optimization_barrier((weight_grad, even_near))
    moved = [paired(weight_grad, "z", step) for step in (4, 12, 8)]
    weight_grad = (weight_grad + moved[2]) + (moved[0] + moved[1])
    feature_grad, output = call(
        spread_own_kernel,
        tables + (grads, even_last, odd_last, *output),
        table_specs + [VMEM] * (3 + n_cols),
        arrays(2, whole),
        scratch=[total],
        flops=18 * tile_flops,
    )
    weight_grad, feature_grad = lax.optimization_barrier((weight_grad, feature_grad))
    weight_grad = summed(weight_grad, ("yh", "x"))
    weight_grad = (weight_grad * (1.0 / (node_count * n_rows) ** 0.5)).T
    return (output.T, feature_grad.T, weight_grad)


def solution(mesh):
    n_rows, n_cols = mesh.shape["rows"], mesh.shape["cols"]
    devices = mesh.devices.reshape(2, n_rows // 8, 4, 2, n_cols // 2)
    fine = Mesh(devices, ROWS + COLS)
    in_specs = (
        P(ROWS, COLS),
        P(None, COLS),
        P(ROWS, None, None),
        P(ROWS),
        P(ROWS),
        P(ROWS),
        P(ROWS, COLS),
    )
    out_specs = (P(ROWS, COLS), P(ROWS, COLS), P(None, COLS))
    return jax.shard_map(local, mesh=fine, in_specs=in_specs, out_specs=out_specs, check_vma=False)
```

```python
import functools

import jax
import jax.numpy as jnp
from jax import lax
from jax.experimental import pallas as pl
from jax.experimental.pallas import tpu as pltpu
from jax.sharding import Mesh, PartitionSpec as P

ROWS = ("yh", "z", "x")
COLS = ("yl", "core")
BLOCK = 128
NEAR = 5
VMEM = pl.BlockSpec(memory_space=pltpu.VMEM)
SMEM = pl.BlockSpec(memory_space=pltpu.SMEM)
BATCH = 6
PARTNERS = (0, 3, 2, 1)


def swap_pairs(count, odd):
    pairs = []
    for first in range(odd, count, 2):
        second = (first + 1) % count
        pairs += [(first, second), (second, first)]
    return pairs


def lanes(index):
    return pl.ds(pl.multiple_of(index * BLOCK, BLOCK), BLOCK)


def wide_lanes(index, width):
    return pl.ds(pl.multiple_of(index * width, width), width)


def each_tile(offset, count, values_ref, term, add):
    slots = values_ref.shape[0]
    per_offset = -(-slots // NEAR)
    for first in range(0, per_offset, BATCH):
        held = []
        for k in range(first, min(first + BATCH, per_offset)):
            slot = k * NEAR + offset
            live = (slot < count).astype(jnp.float32)
            slot = jnp.minimum(slot, slots - 1)
            held.append((slot, term(slot) * live))
        for slot, product in held:
            add(slot, product)


def gather_terms(info, source_ref, total_ref, offset):
    values_ref, rows_ref, cols_ref, count = info
    blocks = source_ref.shape[1] // BLOCK

    def term(slot):
        source = source_ref[:, lanes(lax.rem(cols_ref[slot], blocks))]
        return lax.dot_general(
            source, values_ref[slot], (((1,), (1,)), ((), ())), preferred_element_type=jnp.float32
        )

    def add(slot, product):
        where = lanes(rows_ref[slot])
        total_ref[:, where] = total_ref[:, where] + product

    each_tile(offset, count, values_ref, term, add)


def first_kernel(values, rows, cols, count, place, own, even, total):
    total[...] = jnp.zeros_like(total)
    info = (values, rows, cols, count[0])
    gather_terms(info, own, total, 2)
    gather_terms(info, even, total, 3 - 2 * place[0])


def second_kernel(values, rows, cols, count, place, start, odd, total):
    total[...] = start[...]
    gather_terms((values, rows, cols, count[0]), odd, total, 1 + 2 * place[0])


def pack_kernel(values, rows, cols, count, place, own, cotangent, weight, *packed):
    width = packed[0].shape[1] - weight.shape[1]
    for step, out in enumerate(packed):
        out[:, :width] = cotangent[:, wide_lanes(place[1] ^ PARTNERS[step], width)]
        out[:, width:] = weight[...]


def far_kernel(values, rows, cols, count, place, start, even, odd, *rest):
    hidden, total = rest[:-1], rest[-1]
    total[...] = start[...]
    info = (values, rows, cols, count[0])
    even_offset = 4 - 4 * place[0]
    gather_terms(info, even, total, even_offset)
    gather_terms(info, odd, total, 4 - even_offset)
    for step, out in enumerate(hidden):
        width = out.shape[1]
        out[...] = total[:, wide_lanes(place[1] ^ PARTNERS[step], width)].astype(out.dtype)


def dense_kernel(place, *refs):
    n = (len(refs) - 2) // 4
    hidden, given, sent, output = (refs[k * n : (k + 1) * n] for k in range(4))
    source_ref, back_ref = refs[4 * n :]
    cols, width = hidden[0].shape

    def group(step):
        return pl.ds(pl.multiple_of((place[1] ^ PARTNERS[step]) * cols, cols), cols)

    for step in range(n):
        source_ref[group(step), :] = hidden[step][...]
    source = source_ref[...]
    weight_t = jnp.concatenate([ref[:, width:] for ref in given], 0)
    preact = jnp.dot(weight_t, source, preferred_element_type=jnp.float32)
    sigmoid = 1.0 / (1.0 + jnp.exp(-preact))
    value = (preact * sigmoid).astype(jnp.bfloat16)
    slope = sigmoid * (1.0 + preact * (1.0 - sigmoid))
    grad = jnp.concatenate([ref[:, :width] for ref in given], 0).astype(jnp.float32) * slope
    grad = grad.astype(jnp.bfloat16)
    back = lax.dot_general(
        weight_t, grad, (((0,), (0,)), ((), ())), preferred_element_type=jnp.float32
    )
    back_ref[...] = back.astype(back_ref.dtype)
    weight_term = lax.dot_general(
        grad, source, (((1,), (1,)), ((), ())), preferred_element_type=jnp.float32
    ).astype(jnp.bfloat16)
    for step in range(n):
        here = slice(step * cols, (step + 1) * cols)
        output[step][...] = value[here]
        sent[step][:, :width] = back_ref[group(step), :]
        sent[step][:, width:] = weight_term[here]


def spread_terms(info, grad_ref, total_ref, offset):
    values_ref, rows_ref, cols_ref, count = info
    blocks = total_ref.shape[1] // BLOCK
    per_part = blocks // grad_ref.shape[0]

    def term(slot):
        row = rows_ref[slot]
        part = row // per_part
        source = grad_ref[part, :, lanes(row - part * per_part)]
        return jnp.dot(source, values_ref[slot], preferred_element_type=jnp.float32)

    def add(slot, product):
        where = lanes(lax.rem(cols_ref[slot], blocks))
        total_ref[:, where] = total_ref[:, where] + product

    each_tile(offset, count, values_ref, term, add)


def spread_far_kernel(values, rows, cols, count, place, *refs):
    n = len(refs) - 5
    sent = refs[:n]
    even, odd, grads, even_total, odd_total = refs[n:]
    width = grads.shape[2]
    for step, ref in enumerate(sent):
        grads[place[1] ^ PARTNERS[step]] = ref[:, :width]
    info = (values, rows, cols, count[0])
    even_offset = 4 - 4 * place[0]
    for offset, total, out in ((even_offset, even_total, even), (4 - even_offset, odd_total, odd)):
        total[...] = jnp.zeros_like(total)
        spread_terms(info, grads, total, offset)
        out[...] = total[...].astype(out.dtype)


def spread_near_kernel(offset, sign, values, rows, cols, count, place, grad, received, out, total):
    total[...] = received[...].astype(total.dtype)
    spread_terms((values, rows, cols, count[0]), grad, total, offset + sign * place[0])
    out[...] = total[...].astype(out.dtype)


def spread_own_kernel(values, rows, cols, count, place, grad, from_even, from_odd, *refs):
    parts, (out, output, total) = refs[:-3], refs[-3:]
    info = (values, rows, cols, count[0])
    total[...] = from_even[...].astype(total.dtype) + from_odd[...].astype(total.dtype)
    spread_terms(info, grad, total, 2)
    out[...] = total[...].astype(out.dtype)
    for step, part in enumerate(parts):
        output[:, wide_lanes(place[1] ^ PARTNERS[step], part.shape[1])] = part[...]


def call(kernel, args, specs, outs, scratch=(), flops=0):
    moved = sum(a.size * a.dtype.itemsize for a in args)
    moved += sum(o.size * o.dtype.itemsize for o in outs)
    return pl.pallas_call(
        kernel,
        out_shape=outs,
        in_specs=specs,
        out_specs=[VMEM] * len(outs),
        scratch_shapes=scratch,
        cost_estimate=pl.CostEstimate(flops=flops, bytes_accessed=moved, transcendentals=0),
        compiler_params=pltpu.CompilerParams(vmem_limit_bytes=24 << 20),
    )(*args)


def swapped(values):
    def pairs(step):
        return [(source, source ^ PARTNERS[step]) for source in range(len(values))]

    return [values[0]] + [
        lax.ppermute(value, COLS, pairs(step)) for step, value in enumerate(values) if step
    ]


def summed(value, axis):
    copies = jnp.broadcast_to(value.astype(jnp.bfloat16), (lax.axis_size(axis), *value.shape))
    return lax.all_to_all(copies, axis, 0, 0, tiled=True).astype(jnp.float32).sum(0)


def paired(value, axis, step):
    count = lax.axis_size(axis)
    return lax.ppermute(value, axis, [(source, source ^ step) for source in range(count)])


def local(features, weight, tile_values, tile_rows, tile_cols, tile_count, cotangent):
    node_count, feat_cols = features.shape
    slots, tile, _ = tile_values.shape
    n_rows = lax.axis_size(ROWS)
    n_cols = lax.axis_size(COLS)
    width = node_count // n_cols
    full = feat_cols * n_cols
    even_pairs = swap_pairs(n_rows, 0)
    odd_pairs = swap_pairs(n_rows, 1)

    def even_swap(value):
        return lax.ppermute(value, ROWS, even_pairs)

    def odd_swap(value):
        return lax.ppermute(value, ROWS, odd_pairs)

    place = jnp.stack([lax.rem(lax.axis_index("x"), 2), lax.axis_index(COLS)]).astype(jnp.int32)
    tables = (tile_values, tile_rows, tile_cols, tile_count, place)
    table_specs = [VMEM, SMEM, SMEM, SMEM, SMEM]
    tile_flops = 2 * tile * tile * feat_cols

    def arrays(number, shape, dtype=jnp.bfloat16):
        return [jax.ShapeDtypeStruct(shape, dtype)] * number

    whole = (feat_cols, node_count)
    total = pltpu.VMEM(whole, jnp.float32)

    own = features.T
    even1 = even_swap(own)
    odd1 = odd_swap(own)
    given = call(
        pack_kernel,
        tables + (own, cotangent.T, weight.T),
        table_specs + [VMEM] * 3,
        arrays(n_cols, (feat_cols, width + full)),
    )
    even1, _ = lax.optimization_barrier((even1, given[0]))
    given = swapped(given)
    odd2 = odd_swap(even1)
    (first,) = call(
        first_kernel,
        tables + (own, even1),
        table_specs + [VMEM] * 2,
        arrays(1, whole, jnp.float32),
        flops=36 * tile_flops,
    )
    odd1, first = lax.optimization_barrier((odd1, first))
    even2 = even_swap(odd1)
    (near,) = call(
        second_kernel,
        tables + (first, odd1),
        table_specs + [VMEM] * 2,
        arrays(1, whole, jnp.float32),
        flops=18 * tile_flops,
    )
    hidden = call(
        far_kernel,
        tables + (near, even2, odd2),
        table_specs + [VMEM] * 3,
        arrays(n_cols, (feat_cols, width)),
        scratch=[total],
        flops=36 * tile_flops,
    )
    both = call(
        dense_kernel,
        (place, *swapped(hidden), *given),
        [SMEM] + [VMEM] * (2 * n_cols),
        arrays(n_cols, (feat_cols, width + full)) + arrays(n_cols, (feat_cols, width)),
        scratch=[pltpu.VMEM((full, width), jnp.bfloat16)] * 2,
        flops=6 * full * full * width,
    )
    output, sent = both[n_cols:], swapped(both[:n_cols])
    terms = [value[:, width:].astype(jnp.float32) for value in sent]
    weight_grad = sum(terms[1:], terms[0])
    even_far, odd_far, grads = call(
        spread_far_kernel,
        tables + tuple(sent),
        table_specs + [VMEM] * n_cols,
        arrays(2, whole) + arrays(1, (n_cols, feat_cols, width)),
        scratch=[total, total],
        flops=36 * tile_flops,
    )
    even_in = even_swap(even_far)
    odd_in = odd_swap(odd_far)
    weight_grad, _ = lax.optimization_barrier((weight_grad, even_far))
    weight_grad = weight_grad + paired(weight_grad, "z", 1)
    weight_grad = weight_grad + paired(weight_grad, "z", 2)

    def near_terms(offset, sign, received):
        return call(
            functools.partial(spread_near_kernel, offset, sign),
            tables + (grads, received),
            table_specs + [VMEM] * 2,
            arrays(1, whole),
            scratch=[total],
            flops=18 * tile_flops,
        )[0]

    even_in, _ = lax.optimization_barrier((even_in, weight_grad))
    odd_near = near_terms(1, 2, even_in)
    odd_last = odd_swap(odd_near)
    output = swapped(output)
    odd_in, *_ = lax.optimization_barrier((odd_in, odd_near, *output))
    even_near = near_terms(3, -2, odd_in)
    even_last = even_swap(even_near)
    weight_grad, _ = lax.optimization_barrier((weight_grad, even_near))
    moved = [paired(weight_grad, "z", step) for step in (4, 12, 8)]
    weight_grad = (weight_grad + moved[2]) + (moved[0] + moved[1])
    feature_grad, output = call(
        spread_own_kernel,
        tables + (grads, even_last, odd_last, *output),
        table_specs + [VMEM] * (3 + n_cols),
        arrays(2, whole),
        scratch=[total],
        flops=18 * tile_flops,
    )
    weight_grad, feature_grad = lax.optimization_barrier((weight_grad, feature_grad))
    weight_grad = summed(weight_grad, ("yh", "x"))
    weight_grad = (weight_grad * (1.0 / (node_count * n_rows) ** 0.5)).T
    return (output.T, feature_grad.T, weight_grad)


def solution(mesh):
    n_rows, n_cols = mesh.shape["rows"], mesh.shape["cols"]
    devices = mesh.devices.reshape(2, n_rows // 8, 4, 2, n_cols // 2)
    fine = Mesh(devices, ROWS + COLS)
    in_specs = (
        P(ROWS, COLS),
        P(None, COLS),
        P(ROWS, None, None),
        P(ROWS),
        P(ROWS),
        P(ROWS),
        P(ROWS, COLS),
    )
    out_specs = (P(ROWS, COLS), P(ROWS, COLS), P(None, COLS))
    return jax.shard_map(local, mesh=fine, in_specs=in_specs, out_specs=out_specs, check_vma=False)
```

```python
import functools

import jax
import jax.numpy as jnp
from jax import lax
from jax.experimental import pallas as pl
from jax.experimental.pallas import tpu as pltpu
from jax.sharding import Mesh, PartitionSpec as P

ROWS = ("yh", "z", "x")
COLS = ("yl", "core")
BLOCK = 128
NEAR = 5
VMEM = pl.BlockSpec(memory_space=pltpu.VMEM)
SMEM = pl.BlockSpec(memory_space=pltpu.SMEM)
BATCH = 6
PARTNERS = (0, 3, 2, 1)


def swap_pairs(count, odd):
    pairs = []
    for first in range(odd, count, 2):
        second = (first + 1) % count
        pairs += [(first, second), (second, first)]
    return pairs


def lanes(index):
    return pl.ds(pl.multiple_of(index * BLOCK, BLOCK), BLOCK)


def wide_lanes(index, width):
    return pl.ds(pl.multiple_of(index * width, width), width)


def each_tile(offset, count, values_ref, term, add):
    slots = values_ref.shape[0]
    per_offset = -(-slots // NEAR)
    for first in range(0, per_offset, BATCH):
        held = []
        for k in range(first, min(first + BATCH, per_offset)):
            slot = k * NEAR + offset
            live = (slot < count).astype(jnp.float32)
            slot = jnp.minimum(slot, slots - 1)
            held.append((slot, term(slot) * live))
        for slot, product in held:
            add(slot, product)


def gather_terms(info, source_ref, total_ref, offset):
    values_ref, rows_ref, cols_ref, count = info
    blocks = source_ref.shape[1] // BLOCK

    def term(slot):
        source = source_ref[:, lanes(lax.rem(cols_ref[slot], blocks))]
        return lax.dot_general(
            source, values_ref[slot], (((1,), (1,)), ((), ())), preferred_element_type=jnp.float32
        )

    def add(slot, product):
        where = lanes(rows_ref[slot])
        total_ref[:, where] = total_ref[:, where] + product

    each_tile(offset, count, values_ref, term, add)


def first_kernel(values, rows, cols, count, place, own, even, total):
    total[...] = jnp.zeros_like(total)
    info = (values, rows, cols, count[0])
    gather_terms(info, own, total, 2)
    gather_terms(info, even, total, 3 - 2 * place[0])


def second_kernel(values, rows, cols, count, place, start, odd, total):
    total[...] = start[...]
    gather_terms((values, rows, cols, count[0]), odd, total, 1 + 2 * place[0])


def pack_kernel(values, rows, cols, count, place, own, cotangent, weight, *packed):
    width = packed[0].shape[1] - weight.shape[1]
    for step, out in enumerate(packed):
        out[:, :width] = cotangent[:, wide_lanes(place[1] ^ PARTNERS[step], width)]
        out[:, width:] = weight[...]


def far_kernel(values, rows, cols, count, place, start, even, odd, *rest):
    hidden, total = rest[:-1], rest[-1]
    total[...] = start[...]
    info = (values, rows, cols, count[0])
    even_offset = 4 - 4 * place[0]
    gather_terms(info, even, total, even_offset)
    gather_terms(info, odd, total, 4 - even_offset)
    for step, out in enumerate(hidden):
        width = out.shape[1]
        out[...] = total[:, wide_lanes(place[1] ^ PARTNERS[step], width)].astype(out.dtype)


def dense_kernel(place, *refs):
    n = (len(refs) - 2) // 4
    hidden, given, sent, output = (refs[k * n : (k + 1) * n] for k in range(4))
    source_ref, back_ref = refs[4 * n :]
    cols, width = hidden[0].shape

    def group(step):
        return pl.ds(pl.multiple_of((place[1] ^ PARTNERS[step]) * cols, cols), cols)

    for step in range(n):
        source_ref[group(step), :] = hidden[step][...]
    source = source_ref[...]
    weight_t = jnp.concatenate([ref[:, width:] for ref in given], 0)
    preact = jnp.dot(weight_t, source, preferred_element_type=jnp.float32)
    sigmoid = 1.0 / (1.0 + jnp.exp(-preact))
    value = (preact * sigmoid).astype(jnp.bfloat16)
    slope = sigmoid * (1.0 + preact * (1.0 - sigmoid))
    grad = jnp.concatenate([ref[:, :width] for ref in given], 0).astype(jnp.float32) * slope
    grad = grad.astype(jnp.bfloat16)
    back = lax.dot_general(
        weight_t, grad, (((0,), (0,)), ((), ())), preferred_element_type=jnp.float32
    )
    back_ref[...] = back.astype(back_ref.dtype)
    weight_term = lax.dot_general(
        grad, source, (((1,), (1,)), ((), ())), preferred_element_type=jnp.float32
    ).astype(jnp.bfloat16)
    for step in range(n):
        here = slice(step * cols, (step + 1) * cols)
        output[step][...] = value[here]
        sent[step][:, :width] = back_ref[group(step), :]
        sent[step][:, width:] = weight_term[here]


def spread_terms(info, grad_ref, total_ref, offset):
    values_ref, rows_ref, cols_ref, count = info
    blocks = total_ref.shape[1] // BLOCK
    per_part = blocks // grad_ref.shape[0]

    def term(slot):
        row = rows_ref[slot]
        part = row // per_part
        source = grad_ref[part, :, lanes(row - part * per_part)]
        return jnp.dot(source, values_ref[slot], preferred_element_type=jnp.float32)

    def add(slot, product):
        where = lanes(lax.rem(cols_ref[slot], blocks))
        total_ref[:, where] = total_ref[:, where] + product

    each_tile(offset, count, values_ref, term, add)


def spread_far_kernel(values, rows, cols, count, place, *refs):
    n = len(refs) - 5
    sent = refs[:n]
    even, odd, grads, even_total, odd_total = refs[n:]
    width = grads.shape[2]
    for step, ref in enumerate(sent):
        grads[place[1] ^ PARTNERS[step]] = ref[:, :width]
    info = (values, rows, cols, count[0])
    even_offset = 4 - 4 * place[0]
    for offset, total, out in ((even_offset, even_total, even), (4 - even_offset, odd_total, odd)):
        total[...] = jnp.zeros_like(total)
        spread_terms(info, grads, total, offset)
        out[...] = total[...].astype(out.dtype)


def spread_near_kernel(offset, sign, values, rows, cols, count, place, grad, received, out, total):
    total[...] = received[...].astype(total.dtype)
    spread_terms((values, rows, cols, count[0]), grad, total, offset + sign * place[0])
    out[...] = total[...].astype(out.dtype)


def spread_own_kernel(values, rows, cols, count, place, grad, from_even, from_odd, *refs):
    parts, (out, output, total) = refs[:-3], refs[-3:]
    info = (values, rows, cols, count[0])
    total[...] = from_even[...].astype(total.dtype) + from_odd[...].astype(total.dtype)
    spread_terms(info, grad, total, 2)
    out[...] = total[...].astype(out.dtype)
    for step, part in enumerate(parts):
        output[:, wide_lanes(place[1] ^ PARTNERS[step], part.shape[1])] = part[...]


def call(kernel, args, specs, outs, scratch=(), flops=0):
    moved = sum(a.size * a.dtype.itemsize for a in args)
    moved += sum(o.size * o.dtype.itemsize for o in outs)
    return pl.pallas_call(
        kernel,
        out_shape=outs,
        in_specs=specs,
        out_specs=[VMEM] * len(outs),
        scratch_shapes=scratch,
        cost_estimate=pl.CostEstimate(flops=flops, bytes_accessed=moved, transcendentals=0),
        compiler_params=pltpu.CompilerParams(vmem_limit_bytes=24 << 20),
    )(*args)


def swapped(values):
    def pairs(step):
        return [(source, source ^ PARTNERS[step]) for source in range(len(values))]

    return [values[0]] + [
        lax.ppermute(value, COLS, pairs(step)) for step, value in enumerate(values) if step
    ]


def summed(value, axis):
    copies = jnp.broadcast_to(value.astype(jnp.bfloat16), (lax.axis_size(axis), *value.shape))
    return lax.all_to_all(copies, axis, 0, 0, tiled=True).astype(jnp.float32).sum(0)


def paired(value, axis, step):
    count = lax.axis_size(axis)
    return lax.ppermute(value, axis, [(source, source ^ step) for source in range(count)])


def local(features, weight, tile_values, tile_rows, tile_cols, tile_count, cotangent):
    node_count, feat_cols = features.shape
    slots, tile, _ = tile_values.shape
    n_rows = lax.axis_size(ROWS)
    n_cols = lax.axis_size(COLS)
    width = node_count // n_cols
    full = feat_cols * n_cols
    even_pairs = swap_pairs(n_rows, 0)
    odd_pairs = swap_pairs(n_rows, 1)

    def even_swap(value):
        return lax.ppermute(value, ROWS, even_pairs)

    def odd_swap(value):
        return lax.ppermute(value, ROWS, odd_pairs)

    place = jnp.stack([lax.rem(lax.axis_index("x"), 2), lax.axis_index(COLS)]).astype(jnp.int32)
    tables = (tile_values, tile_rows, tile_cols, tile_count, place)
    table_specs = [VMEM, SMEM, SMEM, SMEM, SMEM]
    tile_flops = 2 * tile * tile * feat_cols

    def arrays(number, shape, dtype=jnp.bfloat16):
        return [jax.ShapeDtypeStruct(shape, dtype)] * number

    whole = (feat_cols, node_count)
    total = pltpu.VMEM(whole, jnp.float32)

    own = features.T
    even1 = even_swap(own)
    odd1 = odd_swap(own)
    given = call(
        pack_kernel,
        tables + (own, cotangent.T, weight.T),
        table_specs + [VMEM] * 3,
        arrays(n_cols, (feat_cols, width + full)),
    )
    even1, _ = lax.optimization_barrier((even1, given[0]))
    given = swapped(given)
    odd2 = odd_swap(even1)
    (first,) = call(
        first_kernel,
        tables + (own, even1),
        table_specs + [VMEM] * 2,
        arrays(1, whole, jnp.float32),
        flops=36 * tile_flops,
    )
    odd1, first = lax.optimization_barrier((odd1, first))
    even2 = even_swap(odd1)
    (near,) = call(
        second_kernel,
        tables + (first, odd1),
        table_specs + [VMEM] * 2,
        arrays(1, whole, jnp.float32),
        flops=18 * tile_flops,
    )
    hidden = call(
        far_kernel,
        tables + (near, even2, odd2),
        table_specs + [VMEM] * 3,
        arrays(n_cols, (feat_cols, width)),
        scratch=[total],
        flops=36 * tile_flops,
    )
    both = call(
        dense_kernel,
        (place, *swapped(hidden), *given),
        [SMEM] + [VMEM] * (2 * n_cols),
        arrays(n_cols, (feat_cols, width + full)) + arrays(n_cols, (feat_cols, width)),
        scratch=[pltpu.VMEM((full, width), jnp.bfloat16)] * 2,
        flops=6 * full * full * width,
    )
    output, sent = both[n_cols:], swapped(both[:n_cols])
    terms = [value[:, width:].astype(jnp.float32) for value in sent]
    weight_grad = sum(terms[1:], terms[0])
    even_far, odd_far, grads = call(
        spread_far_kernel,
        tables + tuple(sent),
        table_specs + [VMEM] * n_cols,
        arrays(2, whole) + arrays(1, (n_cols, feat_cols, width)),
        scratch=[total, total],
        flops=36 * tile_flops,
    )
    weight_grad = weight_grad + paired(weight_grad, "z", 1)
    even_far, odd_far, weight_grad = lax.optimization_barrier((even_far, odd_far, weight_grad))
    even_in = even_swap(even_far)
    odd_in = odd_swap(odd_far)
    weight_grad = weight_grad + paired(weight_grad, "z", 2)

    def near_terms(offset, sign, received):
        return call(
            functools.partial(spread_near_kernel, offset, sign),
            tables + (grads, received),
            table_specs + [VMEM] * 2,
            arrays(1, whole),
            scratch=[total],
            flops=18 * tile_flops,
        )[0]

    even_in, _ = lax.optimization_barrier((even_in, weight_grad))
    odd_near = near_terms(1, 2, even_in)
    odd_last = odd_swap(odd_near)
    output = swapped(output)
    odd_in, *_ = lax.optimization_barrier((odd_in, odd_near, *output))
    even_near = near_terms(3, -2, odd_in)
    even_last = even_swap(even_near)
    weight_grad, _ = lax.optimization_barrier((weight_grad, even_near))
    moved = [paired(weight_grad, "z", step) for step in (4, 12, 8)]
    weight_grad = (weight_grad + moved[2]) + (moved[0] + moved[1])
    feature_grad, output = call(
        spread_own_kernel,
        tables + (grads, even_last, odd_last, *output),
        table_specs + [VMEM] * (3 + n_cols),
        arrays(2, whole),
        scratch=[total],
        flops=18 * tile_flops,
    )
    weight_grad, feature_grad = lax.optimization_barrier((weight_grad, feature_grad))
    weight_grad = summed(weight_grad, ("yh", "x"))
    weight_grad = (weight_grad * (1.0 / (node_count * n_rows) ** 0.5)).T
    return (output.T, feature_grad.T, weight_grad)


def solution(mesh):
    n_rows, n_cols = mesh.shape["rows"], mesh.shape["cols"]
    devices = mesh.devices.reshape(2, n_rows // 8, 4, 2, n_cols // 2)
    fine = Mesh(devices, ROWS + COLS)
    in_specs = (
        P(ROWS, COLS),
        P(None, COLS),
        P(ROWS, None, None),
        P(ROWS),
        P(ROWS),
        P(ROWS),
        P(ROWS, COLS),
    )
    out_specs = (P(ROWS, COLS), P(ROWS, COLS), P(None, COLS))
    return jax.shard_map(local, mesh=fine, in_specs=in_specs, out_specs=out_specs, check_vma=False)
```

```python
import functools

import jax
import jax.numpy as jnp
from jax import lax
from jax.experimental import pallas as pl
from jax.experimental.pallas import tpu as pltpu
from jax.sharding import Mesh, PartitionSpec as P

ROWS = ("yh", "z", "x")
COLS = ("yl", "core")
BLOCK = 128
NEAR = 5
VMEM = pl.BlockSpec(memory_space=pltpu.VMEM)
SMEM = pl.BlockSpec(memory_space=pltpu.SMEM)
BATCH = 6
PARTNERS = (0, 3, 2, 1)


def swap_pairs(count, odd):
    pairs = []
    for first in range(odd, count, 2):
        second = (first + 1) % count
        pairs += [(first, second), (second, first)]
    return pairs


def lanes(index):
    return pl.ds(pl.multiple_of(index * BLOCK, BLOCK), BLOCK)


def wide_lanes(index, width):
    return pl.ds(pl.multiple_of(index * width, width), width)


def each_tile(offset, count, values_ref, term, add):
    slots = values_ref.shape[0]
    per_offset = -(-slots // NEAR)
    for first in range(0, per_offset, BATCH):
        held = []
        for k in range(first, min(first + BATCH, per_offset)):
            slot = k * NEAR + offset
            live = (slot < count).astype(jnp.float32)
            slot = jnp.minimum(slot, slots - 1)
            held.append((slot, term(slot) * live))
        for slot, product in held:
            add(slot, product)


def gather_terms(info, source_ref, total_ref, offset):
    values_ref, rows_ref, cols_ref, count = info
    blocks = source_ref.shape[1] // BLOCK

    def term(slot):
        source = source_ref[:, lanes(lax.rem(cols_ref[slot], blocks))]
        return lax.dot_general(
            source, values_ref[slot], (((1,), (1,)), ((), ())), preferred_element_type=jnp.float32
        )

    def add(slot, product):
        where = lanes(rows_ref[slot])
        total_ref[:, where] = total_ref[:, where] + product

    each_tile(offset, count, values_ref, term, add)


def first_kernel(values, rows, cols, count, place, own, even, total):
    total[...] = jnp.zeros_like(total)
    info = (values, rows, cols, count[0])
    gather_terms(info, own, total, 2)
    gather_terms(info, even, total, 3 - 2 * place[0])


def second_kernel(values, rows, cols, count, place, start, odd, total):
    total[...] = start[...]
    gather_terms((values, rows, cols, count[0]), odd, total, 1 + 2 * place[0])


def pack_kernel(values, rows, cols, count, place, own, cotangent, weight, *packed):
    width = packed[0].shape[1] - weight.shape[1]
    for step, out in enumerate(packed):
        out[:, :width] = cotangent[:, wide_lanes(place[1] ^ PARTNERS[step], width)]
        out[:, width:] = weight[...]


def far_kernel(values, rows, cols, count, place, start, even, odd, *rest):
    hidden, total = rest[:-1], rest[-1]
    total[...] = start[...]
    info = (values, rows, cols, count[0])
    even_offset = 4 - 4 * place[0]
    gather_terms(info, even, total, even_offset)
    gather_terms(info, odd, total, 4 - even_offset)
    for step, out in enumerate(hidden):
        width = out.shape[1]
        out[...] = total[:, wide_lanes(place[1] ^ PARTNERS[step], width)].astype(out.dtype)


def dense_kernel(place, *refs):
    n = (len(refs) - 2) // 4
    hidden, given, sent, output = (refs[k * n : (k + 1) * n] for k in range(4))
    source_ref, back_ref = refs[4 * n :]
    cols, width = hidden[0].shape

    def group(step):
        return pl.ds(pl.multiple_of((place[1] ^ PARTNERS[step]) * cols, cols), cols)

    for step in range(n):
        source_ref[group(step), :] = hidden[step][...]
    source = source_ref[...]
    weight_t = jnp.concatenate([ref[:, width:] for ref in given], 0)
    preact = jnp.dot(weight_t, source, preferred_element_type=jnp.float32)
    sigmoid = 1.0 / (1.0 + jnp.exp(-preact))
    value = (preact * sigmoid).astype(jnp.bfloat16)
    slope = sigmoid * (1.0 + preact * (1.0 - sigmoid))
    grad = jnp.concatenate([ref[:, :width] for ref in given], 0).astype(jnp.float32) * slope
    grad = grad.astype(jnp.bfloat16)
    back = lax.dot_general(
        weight_t, grad, (((0,), (0,)), ((), ())), preferred_element_type=jnp.float32
    )
    back_ref[...] = back.astype(back_ref.dtype)
    weight_term = lax.dot_general(
        grad, source, (((1,), (1,)), ((), ())), preferred_element_type=jnp.float32
    ).astype(jnp.bfloat16)
    for step in range(n):
        here = slice(step * cols, (step + 1) * cols)
        output[step][...] = value[here]
        sent[step][:, :width] = back_ref[group(step), :]
        sent[step][:, width:] = weight_term[here]


def spread_terms(info, grad_ref, total_ref, offset):
    values_ref, rows_ref, cols_ref, count = info
    blocks = total_ref.shape[1] // BLOCK
    per_part = blocks // grad_ref.shape[0]

    def term(slot):
        row = rows_ref[slot]
        part = row // per_part
        source = grad_ref[part, :, lanes(row - part * per_part)]
        return jnp.dot(source, values_ref[slot], preferred_element_type=jnp.float32)

    def add(slot, product):
        where = lanes(lax.rem(cols_ref[slot], blocks))
        total_ref[:, where] = total_ref[:, where] + product

    each_tile(offset, count, values_ref, term, add)


def spread_far_kernel(values, rows, cols, count, place, *refs):
    n = len(refs) - 5
    sent = refs[:n]
    even, odd, grads, even_total, odd_total = refs[n:]
    width = grads.shape[2]
    for step, ref in enumerate(sent):
        grads[place[1] ^ PARTNERS[step]] = ref[:, :width]
    info = (values, rows, cols, count[0])
    even_offset = 4 - 4 * place[0]
    for offset, total, out in ((even_offset, even_total, even), (4 - even_offset, odd_total, odd)):
        total[...] = jnp.zeros_like(total)
        spread_terms(info, grads, total, offset)
        out[...] = total[...].astype(out.dtype)


def spread_near_kernel(offset, sign, values, rows, cols, count, place, grad, received, out, total):
    total[...] = received[...].astype(total.dtype)
    spread_terms((values, rows, cols, count[0]), grad, total, offset + sign * place[0])
    out[...] = total[...].astype(out.dtype)


def spread_own_kernel(values, rows, cols, count, place, grad, from_even, from_odd, *refs):
    parts, (out, output, total) = refs[:-3], refs[-3:]
    info = (values, rows, cols, count[0])
    total[...] = from_even[...].astype(total.dtype) + from_odd[...].astype(total.dtype)
    spread_terms(info, grad, total, 2)
    out[...] = total[...].astype(out.dtype)
    for step, part in enumerate(parts):
        output[:, wide_lanes(place[1] ^ PARTNERS[step], part.shape[1])] = part[...]


def call(kernel, args, specs, outs, scratch=(), flops=0):
    moved = sum(a.size * a.dtype.itemsize for a in args)
    moved += sum(o.size * o.dtype.itemsize for o in outs)
    return pl.pallas_call(
        kernel,
        out_shape=outs,
        in_specs=specs,
        out_specs=[VMEM] * len(outs),
        scratch_shapes=scratch,
        cost_estimate=pl.CostEstimate(flops=flops, bytes_accessed=moved, transcendentals=0),
        compiler_params=pltpu.CompilerParams(vmem_limit_bytes=24 << 20),
    )(*args)


def swapped(values):
    def pairs(step):
        return [(source, source ^ PARTNERS[step]) for source in range(len(values))]

    return [values[0]] + [
        lax.ppermute(value, COLS, pairs(step)) for step, value in enumerate(values) if step
    ]


def summed(value, axis):
    copies = jnp.broadcast_to(value.astype(jnp.bfloat16), (lax.axis_size(axis), *value.shape))
    return lax.all_to_all(copies, axis, 0, 0, tiled=True).astype(jnp.float32).sum(0)


def paired(value, axis, step):
    count = lax.axis_size(axis)
    return lax.ppermute(value, axis, [(source, source ^ step) for source in range(count)])


def local(features, weight, tile_values, tile_rows, tile_cols, tile_count, cotangent):
    node_count, feat_cols = features.shape
    slots, tile, _ = tile_values.shape
    n_rows = lax.axis_size(ROWS)
    n_cols = lax.axis_size(COLS)
    width = node_count // n_cols
    full = feat_cols * n_cols
    even_pairs = swap_pairs(n_rows, 0)
    odd_pairs = swap_pairs(n_rows, 1)

    def even_swap(value):
        return lax.ppermute(value, ROWS, even_pairs)

    def odd_swap(value):
        return lax.ppermute(value, ROWS, odd_pairs)

    place = jnp.stack([lax.rem(lax.axis_index("x"), 2), lax.axis_index(COLS)]).astype(jnp.int32)
    tables = (tile_values, tile_rows, tile_cols, tile_count, place)
    table_specs = [VMEM, SMEM, SMEM, SMEM, SMEM]
    tile_flops = 2 * tile * tile * feat_cols

    def arrays(number, shape, dtype=jnp.bfloat16):
        return [jax.ShapeDtypeStruct(shape, dtype)] * number

    whole = (feat_cols, node_count)
    total = pltpu.VMEM(whole, jnp.float32)

    own = features.T
    even1 = even_swap(own)
    odd1 = odd_swap(own)
    given = call(
        pack_kernel,
        tables + (own, cotangent.T, weight.T),
        table_specs + [VMEM] * 3,
        arrays(n_cols, (feat_cols, width + full)),
    )
    even1, _ = lax.optimization_barrier((even1, given[0]))
    given = swapped(given)
    odd2 = odd_swap(even1)
    (first,) = call(
        first_kernel,
        tables + (own, even1),
        table_specs + [VMEM] * 2,
        arrays(1, whole, jnp.float32),
        flops=36 * tile_flops,
    )
    odd1, first = lax.optimization_barrier((odd1, first))
    even2 = even_swap(odd1)
    (near,) = call(
        second_kernel,
        tables + (first, odd1),
        table_specs + [VMEM] * 2,
        arrays(1, whole, jnp.float32),
        flops=18 * tile_flops,
    )
    hidden = call(
        far_kernel,
        tables + (near, even2, odd2),
        table_specs + [VMEM] * 3,
        arrays(n_cols, (feat_cols, width)),
        scratch=[total],
        flops=36 * tile_flops,
    )
    both = call(
        dense_kernel,
        (place, *swapped(hidden), *given),
        [SMEM] + [VMEM] * (2 * n_cols),
        arrays(n_cols, (feat_cols, width + full)) + arrays(n_cols, (feat_cols, width)),
        scratch=[pltpu.VMEM((full, width), jnp.bfloat16)] * 2,
        flops=6 * full * full * width,
    )
    output, sent = both[n_cols:], swapped(both[:n_cols])
    terms = [value[:, width:].astype(jnp.float32) for value in sent]
    weight_grad = sum(terms[1:], terms[0])
    even_far, odd_far, grads = call(
        spread_far_kernel,
        tables + tuple(sent),
        table_specs + [VMEM] * n_cols,
        arrays(2, whole) + arrays(1, (n_cols, feat_cols, width)),
        scratch=[total, total],
        flops=36 * tile_flops,
    )
    weight_grad = weight_grad + paired(weight_grad, "z", 1)
    even_far, odd_far, weight_grad = lax.optimization_barrier((even_far, odd_far, weight_grad))
    even_in = even_swap(even_far)
    odd_in = odd_swap(odd_far)
    weight_grad = weight_grad + paired(weight_grad, "z", 2)

    def near_terms(offset, sign, received):
        return call(
            functools.partial(spread_near_kernel, offset, sign),
            tables + (grads, received),
            table_specs + [VMEM] * 2,
            arrays(1, whole),
            scratch=[total],
            flops=18 * tile_flops,
        )[0]

    even_in, _ = lax.optimization_barrier((even_in, weight_grad))
    odd_near = near_terms(1, 2, even_in)
    odd_last = odd_swap(odd_near)
    output = swapped(output)
    odd_in, _ = lax.optimization_barrier((odd_in, odd_near))
    even_near = near_terms(3, -2, odd_in)
    even_near, *_ = lax.optimization_barrier((even_near, *output))
    even_last = even_swap(even_near)
    weight_grad, _ = lax.optimization_barrier((weight_grad, even_near))
    moved = [paired(weight_grad, "z", step) for step in (4, 12, 8)]
    weight_grad = (weight_grad + moved[2]) + (moved[0] + moved[1])
    feature_grad, output = call(
        spread_own_kernel,
        tables + (grads, even_last, odd_last, *output),
        table_specs + [VMEM] * (3 + n_cols),
        arrays(2, whole),
        scratch=[total],
        flops=18 * tile_flops,
    )
    weight_grad, feature_grad = lax.optimization_barrier((weight_grad, feature_grad))
    weight_grad = summed(weight_grad, ("yh", "x"))
    weight_grad = (weight_grad * (1.0 / (node_count * n_rows) ** 0.5)).T
    return (output.T, feature_grad.T, weight_grad)


def solution(mesh):
    n_rows, n_cols = mesh.shape["rows"], mesh.shape["cols"]
    devices = mesh.devices.reshape(2, n_rows // 8, 4, 2, n_cols // 2)
    fine = Mesh(devices, ROWS + COLS)
    in_specs = (
        P(ROWS, COLS),
        P(None, COLS),
        P(ROWS, None, None),
        P(ROWS),
        P(ROWS),
        P(ROWS),
        P(ROWS, COLS),
    )
    out_specs = (P(ROWS, COLS), P(ROWS, COLS), P(None, COLS))
    return jax.shard_map(local, mesh=fine, in_specs=in_specs, out_specs=out_specs, check_vma=False)
```

```python
import functools

import jax
import jax.numpy as jnp
from jax import lax
from jax.experimental import pallas as pl
from jax.experimental.pallas import tpu as pltpu
from jax.sharding import Mesh, PartitionSpec as P

ROWS = ("yh", "z", "x")
COLS = ("yl", "core")
BLOCK = 128
NEAR = 5
VMEM = pl.BlockSpec(memory_space=pltpu.VMEM)
SMEM = pl.BlockSpec(memory_space=pltpu.SMEM)
BATCH = 6
PARTNERS = (0, 3, 2, 1)


def swap_pairs(count, odd):
    pairs = []
    for first in range(odd, count, 2):
        second = (first + 1) % count
        pairs += [(first, second), (second, first)]
    return pairs


def lanes(index):
    return pl.ds(pl.multiple_of(index * BLOCK, BLOCK), BLOCK)


def wide_lanes(index, width):
    return pl.ds(pl.multiple_of(index * width, width), width)


def each_tile(offset, count, values_ref, term, add):
    slots = values_ref.shape[0]
    per_offset = -(-slots // NEAR)
    for first in range(0, per_offset, BATCH):
        held = []
        for k in range(first, min(first + BATCH, per_offset)):
            slot = k * NEAR + offset
            live = (slot < count).astype(jnp.float32)
            slot = jnp.minimum(slot, slots - 1)
            held.append((slot, term(slot) * live))
        for slot, product in held:
            add(slot, product)


def gather_terms(info, source_ref, total_ref, offset):
    values_ref, rows_ref, cols_ref, count = info
    blocks = source_ref.shape[1] // BLOCK

    def term(slot):
        source = source_ref[:, lanes(lax.rem(cols_ref[slot], blocks))]
        return lax.dot_general(
            source, values_ref[slot], (((1,), (1,)), ((), ())), preferred_element_type=jnp.float32
        )

    def add(slot, product):
        where = lanes(rows_ref[slot])
        total_ref[:, where] = total_ref[:, where] + product

    each_tile(offset, count, values_ref, term, add)


def first_kernel(values, rows, cols, count, place, own, even, total):
    total[...] = jnp.zeros_like(total)
    info = (values, rows, cols, count[0])
    gather_terms(info, own, total, 2)
    gather_terms(info, even, total, 3 - 2 * place[0])


def second_kernel(values, rows, cols, count, place, start, odd, total):
    total[...] = start[...]
    gather_terms((values, rows, cols, count[0]), odd, total, 1 + 2 * place[0])


def pack_kernel(values, rows, cols, count, place, own, cotangent, weight, *packed):
    width = packed[0].shape[1] - weight.shape[1]
    for step, out in enumerate(packed):
        out[:, :width] = cotangent[:, wide_lanes(place[1] ^ PARTNERS[step], width)]
        out[:, width:] = weight[...]


def far_kernel(values, rows, cols, count, place, start, even, odd, *rest):
    hidden, total = rest[:-1], rest[-1]
    total[...] = start[...]
    info = (values, rows, cols, count[0])
    even_offset = 4 - 4 * place[0]
    gather_terms(info, even, total, even_offset)
    gather_terms(info, odd, total, 4 - even_offset)
    for step, out in enumerate(hidden):
        width = out.shape[1]
        out[...] = total[:, wide_lanes(place[1] ^ PARTNERS[step], width)].astype(out.dtype)


def dense_kernel(place, *refs):
    n = (len(refs) - 2) // 4
    hidden, given, sent, output = (refs[k * n : (k + 1) * n] for k in range(4))
    source_ref, back_ref = refs[4 * n :]
    cols, width = hidden[0].shape

    def group(step):
        return pl.ds(pl.multiple_of((place[1] ^ PARTNERS[step]) * cols, cols), cols)

    for step in range(n):
        source_ref[group(step), :] = hidden[step][...]
    source = source_ref[...]
    weight_t = jnp.concatenate([ref[:, width:] for ref in given], 0)
    preact = jnp.dot(weight_t, source, preferred_element_type=jnp.float32)
    sigmoid = 1.0 / (1.0 + jnp.exp(-preact))
    value = (preact * sigmoid).astype(jnp.bfloat16)
    slope = sigmoid * (1.0 + preact * (1.0 - sigmoid))
    grad = jnp.concatenate([ref[:, :width] for ref in given], 0).astype(jnp.float32) * slope
    grad = grad.astype(jnp.bfloat16)
    back = lax.dot_general(
        weight_t, grad, (((0,), (0,)), ((), ())), preferred_element_type=jnp.float32
    )
    back_ref[...] = back.astype(back_ref.dtype)
    weight_term = lax.dot_general(
        grad, source, (((1,), (1,)), ((), ())), preferred_element_type=jnp.float32
    ).astype(jnp.bfloat16)
    for step in range(n):
        here = slice(step * cols, (step + 1) * cols)
        output[step][...] = value[here]
        sent[step][:, :width] = back_ref[group(step), :]
        sent[step][:, width:] = weight_term[here]


def spread_terms(info, grad_ref, total_ref, offset):
    values_ref, rows_ref, cols_ref, count = info
    blocks = total_ref.shape[1] // BLOCK
    per_part = blocks // grad_ref.shape[0]

    def term(slot):
        row = rows_ref[slot]
        part = row // per_part
        source = grad_ref[part, :, lanes(row - part * per_part)]
        return jnp.dot(source, values_ref[slot], preferred_element_type=jnp.float32)

    def add(slot, product):
        where = lanes(lax.rem(cols_ref[slot], blocks))
        total_ref[:, where] = total_ref[:, where] + product

    each_tile(offset, count, values_ref, term, add)


def spread_far_kernel(values, rows, cols, count, place, *refs):
    n = len(refs) - 5
    sent = refs[:n]
    even, odd, grads, even_total, odd_total = refs[n:]
    width = grads.shape[2]
    for step, ref in enumerate(sent):
        grads[place[1] ^ PARTNERS[step]] = ref[:, :width]
    info = (values, rows, cols, count[0])
    even_offset = 4 - 4 * place[0]
    for offset, total, out in ((even_offset, even_total, even), (4 - even_offset, odd_total, odd)):
        total[...] = jnp.zeros_like(total)
        spread_terms(info, grads, total, offset)
        out[...] = total[...].astype(out.dtype)


def spread_near_kernel(offset, sign, values, rows, cols, count, place, grad, received, out, total):
    total[...] = received[...].astype(total.dtype)
    spread_terms((values, rows, cols, count[0]), grad, total, offset + sign * place[0])
    out[...] = total[...].astype(out.dtype)


def spread_own_kernel(values, rows, cols, count, place, grad, from_even, from_odd, *refs):
    parts, (out, output, total) = refs[:-3], refs[-3:]
    info = (values, rows, cols, count[0])
    total[...] = from_even[...].astype(total.dtype) + from_odd[...].astype(total.dtype)
    spread_terms(info, grad, total, 2)
    out[...] = total[...].astype(out.dtype)
    for step, part in enumerate(parts):
        output[:, wide_lanes(place[1] ^ PARTNERS[step], part.shape[1])] = part[...]


def call(kernel, args, specs, outs, scratch=(), flops=0):
    moved = sum(a.size * a.dtype.itemsize for a in args)
    moved += sum(o.size * o.dtype.itemsize for o in outs)
    return pl.pallas_call(
        kernel,
        out_shape=outs,
        in_specs=specs,
        out_specs=[VMEM] * len(outs),
        scratch_shapes=scratch,
        cost_estimate=pl.CostEstimate(flops=flops, bytes_accessed=moved, transcendentals=0),
        compiler_params=pltpu.CompilerParams(vmem_limit_bytes=24 << 20),
    )(*args)


def swapped(values):
    def pairs(step):
        return [(source, source ^ PARTNERS[step]) for source in range(len(values))]

    return [values[0]] + [
        lax.ppermute(value, COLS, pairs(step)) for step, value in enumerate(values) if step
    ]


def summed(value, axis):
    copies = jnp.broadcast_to(value.astype(jnp.bfloat16), (lax.axis_size(axis), *value.shape))
    return lax.all_to_all(copies, axis, 0, 0, tiled=True).astype(jnp.float32).sum(0)


def paired(value, axis, step):
    count = lax.axis_size(axis)
    return lax.ppermute(value, axis, [(source, source ^ step) for source in range(count)])


def local(features, weight, tile_values, tile_rows, tile_cols, tile_count, cotangent):
    node_count, feat_cols = features.shape
    slots, tile, _ = tile_values.shape
    n_rows = lax.axis_size(ROWS)
    n_cols = lax.axis_size(COLS)
    width = node_count // n_cols
    full = feat_cols * n_cols
    even_pairs = swap_pairs(n_rows, 0)
    odd_pairs = swap_pairs(n_rows, 1)

    def even_swap(value):
        return lax.ppermute(value, ROWS, even_pairs)

    def odd_swap(value):
        return lax.ppermute(value, ROWS, odd_pairs)

    place = jnp.stack([lax.rem(lax.axis_index("x"), 2), lax.axis_index(COLS)]).astype(jnp.int32)
    tables = (tile_values, tile_rows, tile_cols, tile_count, place)
    table_specs = [VMEM, SMEM, SMEM, SMEM, SMEM]
    tile_flops = 2 * tile * tile * feat_cols

    def arrays(number, shape, dtype=jnp.bfloat16):
        return [jax.ShapeDtypeStruct(shape, dtype)] * number

    whole = (feat_cols, node_count)
    total = pltpu.VMEM(whole, jnp.float32)

    own = features.T
    even1 = even_swap(own)
    odd1 = odd_swap(own)
    given = call(
        pack_kernel,
        tables + (own, cotangent.T, weight.T),
        table_specs + [VMEM] * 3,
        arrays(n_cols, (feat_cols, width + full)),
    )
    even1, _ = lax.optimization_barrier((even1, given[0]))
    given = swapped(given)
    odd2 = odd_swap(even1)
    (first,) = call(
        first_kernel,
        tables + (own, even1),
        table_specs + [VMEM] * 2,
        arrays(1, whole, jnp.float32),
        flops=36 * tile_flops,
    )
    odd1, first = lax.optimization_barrier((odd1, first))
    even2 = even_swap(odd1)
    (near,) = call(
        second_kernel,
        tables + (first, odd1),
        table_specs + [VMEM] * 2,
        arrays(1, whole, jnp.float32),
        flops=18 * tile_flops,
    )
    hidden = call(
        far_kernel,
        tables + (near, even2, odd2),
        table_specs + [VMEM] * 3,
        arrays(n_cols, (feat_cols, width)),
        scratch=[total],
        flops=36 * tile_flops,
    )
    both = call(
        dense_kernel,
        (place, *swapped(hidden), *given),
        [SMEM] + [VMEM] * (2 * n_cols),
        arrays(n_cols, (feat_cols, width + full)) + arrays(n_cols, (feat_cols, width)),
        scratch=[pltpu.VMEM((full, width), jnp.bfloat16)] * 2,
        flops=6 * full * full * width,
    )
    output, sent = both[n_cols:], swapped(both[:n_cols])
    terms = [value[:, width:].astype(jnp.float32) for value in sent]
    weight_grad = sum(terms[1:], terms[0])
    even_far, odd_far, grads = call(
        spread_far_kernel,
        tables + tuple(sent),
        table_specs + [VMEM] * n_cols,
        arrays(2, whole) + arrays(1, (n_cols, feat_cols, width)),
        scratch=[total, total],
        flops=36 * tile_flops,
    )
    even_in = even_swap(even_far)
    odd_in = odd_swap(odd_far)
    weight_grad, _ = lax.optimization_barrier((weight_grad, even_far))
    weight_grad = weight_grad + paired(weight_grad, "z", 1)
    weight_grad = weight_grad + paired(weight_grad, "z", 2)

    def near_terms(offset, sign, received):
        return call(
            functools.partial(spread_near_kernel, offset, sign),
            tables + (grads, received),
            table_specs + [VMEM] * 2,
            arrays(1, whole),
            scratch=[total],
            flops=18 * tile_flops,
        )[0]

    even_in, _ = lax.optimization_barrier((even_in, weight_grad))
    odd_near = near_terms(1, 2, even_in)
    odd_last = odd_swap(odd_near)
    output = swapped(output)
    odd_in, _ = lax.optimization_barrier((odd_in, odd_near))
    even_near = near_terms(3, -2, odd_in)
    even_near, *_ = lax.optimization_barrier((even_near, *output))
    even_last = even_swap(even_near)
    weight_grad, _ = lax.optimization_barrier((weight_grad, even_near))
    moved = [paired(weight_grad, "z", step) for step in (4, 12, 8)]
    weight_grad = (weight_grad + moved[2]) + (moved[0] + moved[1])
    feature_grad, output = call(
        spread_own_kernel,
        tables + (grads, even_last, odd_last, *output),
        table_specs + [VMEM] * (3 + n_cols),
        arrays(2, whole),
        scratch=[total],
        flops=18 * tile_flops,
    )
    weight_grad, feature_grad = lax.optimization_barrier((weight_grad, feature_grad))
    weight_grad = summed(weight_grad, ("yh", "x"))
    weight_grad = (weight_grad * (1.0 / (node_count * n_rows) ** 0.5)).T
    return (output.T, feature_grad.T, weight_grad)


def solution(mesh):
    n_rows, n_cols = mesh.shape["rows"], mesh.shape["cols"]
    devices = mesh.devices.reshape(2, n_rows // 8, 4, 2, n_cols // 2)
    fine = Mesh(devices, ROWS + COLS)
    in_specs = (
        P(ROWS, COLS),
        P(None, COLS),
        P(ROWS, None, None),
        P(ROWS),
        P(ROWS),
        P(ROWS),
        P(ROWS, COLS),
    )
    out_specs = (P(ROWS, COLS), P(ROWS, COLS), P(None, COLS))
    return jax.shard_map(local, mesh=fine, in_specs=in_specs, out_specs=out_specs, check_vma=False)
```
